32 devices in a mesh: req: 16 (over z, y, x), blk: 2 (over core).
Axes of the slice: x: 2, y: 2, z: 4, core: 2. Of those that a mesh axis runs over, the one named last changes fastest.
Arguments:
- hidden: bfloat16 [16, 1600], P('req'), may hold values from -6 to 6
- slot_request: int32 [16], replicated, may hold values from 0 to 15, each once
- cache_length: int32 [16], P('req'), may hold values from 1 to 2048, 4096 in all
- block_keep: int32 [16, 16], P('req', 'blk'), may hold values 0 or 1
- stored_keys: bfloat16 [16, 2048, 320], P('req', 'blk'), may hold values from -540 to 540
- stored_values: bfloat16 [16, 2048, 320], P('req', 'blk'), may hold values from -6 to 6
- ssm_state: float32 [16, 16, 3200], P('req', None, 'blk'), may hold values from -6 to 6
- norm_gain: float32 [1600], replicated, may hold values from 0.5 to 1.5
- query_key_value_weight: bfloat16 [1600, 2240], P('blk'), may hold values from -0.15625 to 0.15625
- w_attn_out: bfloat16 [1600, 1600], P('blk'), may hold values from -0.15625 to 0.15625
- mamba_in: bfloat16 [2, 1600, 3200], P(None, None, 'blk'), may hold values from -0.15625 to 0.15625
- select_proj: bfloat16 [3200, 132], P('blk'), may hold values from -0.109375 to 0.109375
- step_proj: bfloat16 [100, 3200], P(None, 'blk'), may hold values from -0.625 to 0.625
- step_bias: float32 [3200], P('blk'), may hold values from -3 to 0.5
- decay_log: float32 [16, 3200], P(None, 'blk'), may hold values from 0 to 2.8
- skip_gain: float32 [3200], P('blk'), may hold values from 0.5 to 1.5
- w_mamba_out: bfloat16 [3200, 1600], P('blk'), may hold values from -0.109375 to 0.109375
- ffn_gain: float32 [1600], replicated, may hold values from 0.5 to 1.5
- w_gate_up: bfloat16 [2, 1600, 5504], P(None, None, 'blk'), may hold values from -0.15625 to 0.15625
- w_down: bfloat16 [5504, 1600], P('blk'), may hold values from -0.078125 to 0.078125
Outputs:
- hidden_out: bfloat16 [16, 1600], P('req', 'blk')
- fresh_entry: bfloat16 [16, 640], P('req')
- new_state: float32 [16, 16, 3200], P('req', None, 'blk')
The draws below stay inside these ranges and needn't reach their ends.
Inputs may be any that keep to these rules, and one draw needn't show every extreme that they name: `slot_request`: each request stands in exactly one slot.
All inputs are finite; a program needn't handle non-finite values. No bound on the sum of `cache_length` or of `block_keep` on one device may be relied on, other than what follows from the above.
Results may differ from the reference program's by a relative error of at most 0.0085.
Values may be sent and summed in bfloat16 or wider, within the bound.
A program may use at most 128 MiB of HBM per device.

```python
import math
import jax
import jax.numpy as jnp
import numpy as np
from jax import lax

MODEL_WIDTH = 1600
QUERY_HEADS = 25
HEAD_SIZE = 64
KEY_HEADS = 5
MI = 3200
NS = 16
RANK = 100
FF = 5504
BLOCK_POSITIONS = 128
REQUEST_COUNT = 16
REQUEST_BLOCKS = 16
REQUEST_LENGTH = 2048


def draw_stored_keys(key, part):
    first_block = jax.random.fold_in(key, 0)
    base_offset = jnp.clip(jax.random.normal(first_block, (REQUEST_COUNT, REQUEST_LENGTH, KEY_HEADS * HEAD_SIZE), jnp.float32), -6.0, 6.0)
    return base_offset.astype(jnp.bfloat16)


def place_ends(result, stream_key, low, top_value):
    spot = [jax.random.randint(jax.random.fold_in(stream_key, axis), (), 0, length) for axis, length in enumerate(result.shape)]
    main_axis = result.shape.index(max(result.shape))
    beside = spot[:main_axis] + [(spot[main_axis] + 1) % result.shape[main_axis]] + spot[main_axis + 1:]
    return result.at[tuple(spot)].set(low).at[tuple(beside)].set(top_value)


def level_of(stream_key, shape, cuts, least, top_value):
    level, own = 1.0, jax.random.fold_in(stream_key, 6)
    for dim, blocks in cuts:
        draws = jnp.exp(jax.random.uniform(jax.random.fold_in(own, dim), (blocks,), jnp.float32, least / len(cuts), top_value / len(cuts)))
        level = level * jnp.repeat(draws, shape[dim] // blocks).reshape([-1 if axis == dim else 1 for axis in range(len(shape))])
    return level


def length_profile(amount, total, reach, slope):
    portions = [(1 << 20) // math.isqrt(standing ** slope) + 1 for standing in range(2, amount + 1)]
    spare, counts = total - reach - (amount - 1), [1] * (amount - 1)
    while spare > 0:
        candidates = [i for i in range(amount - 1) if counts[i] < reach]
        mass, budget = sum([portions[i] for i in candidates]), spare
        for i in candidates:
            more = min(reach - counts[i], max(1, budget * portions[i] // mass), spare)
            counts[i] = counts[i] + more
            spare = spare - more
    return np.array([reach] + counts)


def uneven_parts(rng, amount, total, most, slope):
    if amount == 2:
        one = jax.random.randint(rng, (), max(1, total - most), min(most, total - 1) + 1)
        return jnp.stack([one, total - one])
    lengths = jnp.asarray(length_profile(amount, total, most, slope), jnp.int32)
    pairs = (amount - 1) // 2
    source_of, receiver = lengths[1:1 + 2 * pairs:2], lengths[2:2 + 2 * pairs:2]
    slack = jnp.minimum(source_of - 1, most - receiver)
    passed = jax.random.randint(jax.random.fold_in(rng, 1), (pairs,), 0, 1 << 20) % (slack + 1)
    lengths = lengths.at[1:1 + 2 * pairs:2].set(source_of - passed).at[2:2 + 2 * pairs:2].set(receiver + passed)
    return lengths[jax.random.permutation(jax.random.fold_in(rng, 2), amount)]


def centred(stream_key, shape, spread, reach, cuts=(), kind=jnp.bfloat16):
    result = spread * jax.random.normal(stream_key, shape, jnp.float32)
    if cuts:
        result = result * level_of(stream_key, shape, cuts, -0.22, 0.18)
    return jnp.clip(result, -reach, reach).astype(kind)


def setup_inputs(seed: int = 0) -> dict:
    splits = jax.random.split(jax.random.key(seed), 21)
    return {
        "hidden": centred(splits[0], (REQUEST_COUNT, MODEL_WIDTH), 1.0, 6.0, ((0, 16),)),
        "slot_request": jax.random.permutation(splits[1], REQUEST_COUNT).astype(jnp.int32),
        "cache_length": uneven_parts(splits[2], REQUEST_COUNT, REQUEST_COUNT * REQUEST_LENGTH // 8, REQUEST_LENGTH, 2).astype(jnp.int32),
        "block_keep": place_ends((jax.random.randint(splits[3], (REQUEST_COUNT, REQUEST_BLOCKS), 0, 4) < 3).astype(jnp.int32), jax.random.fold_in(splits[3], 1), 0, 1),
        "stored_keys": draw_stored_keys(jax.random.fold_in(splits[20], 71), 0),
        "stored_values": centred(splits[5], (REQUEST_COUNT, REQUEST_LENGTH, KEY_HEADS * HEAD_SIZE), 1.0, 6.0, ((0, 16), (1, 2))),
        "ssm_state": centred(splits[6], (REQUEST_COUNT, NS, MI), 1.0, 6.0, ((0, 16), (2, 2)), jnp.float32),
        "norm_gain": jnp.clip(jax.random.uniform(splits[7], (MODEL_WIDTH,), jnp.float32, 0.5, 1.5), 0.5, 1.5),
        "query_key_value_weight": centred(splits[8], (MODEL_WIDTH, QUERY_HEADS * HEAD_SIZE + 2 * KEY_HEADS * HEAD_SIZE), MODEL_WIDTH ** -0.5, 0.15625, ((0, 2),)),
        "w_attn_out": centred(splits[9], (QUERY_HEADS * HEAD_SIZE, MODEL_WIDTH), (QUERY_HEADS * HEAD_SIZE) ** -0.5, 0.15625, ((0, 2),)),
        "mamba_in": centred(splits[10], (2, MODEL_WIDTH, MI), MODEL_WIDTH ** -0.5, 0.15625, ((2, 2),)),
        "select_proj": centred(splits[11], (MI, RANK + 2 * NS), MI ** -0.5, 0.109375, ((0, 2),)),
        "step_proj": centred(splits[12], (RANK, MI), RANK ** -0.5, 0.625, ((1, 2),)),
        "step_bias": jnp.clip(-3.0 + 3.5 * jax.random.uniform(splits[13], (MI,), jnp.float32) ** level_of(splits[13], (MI,), ((0, 2),), -0.2, 0.2), -3.0, 0.5),
        "decay_log": jnp.clip(2.8 * jax.random.uniform(splits[14], (NS, MI), jnp.float32) ** level_of(splits[14], (NS, MI), ((1, 2),), -0.2, 0.2), 0.0, 2.8),
        "skip_gain": jnp.clip(0.5 + 1.0 * jax.random.uniform(splits[15], (MI,), jnp.float32) ** level_of(splits[15], (MI,), ((0, 2),), -0.2, 0.2), 0.5, 1.5),
        "w_mamba_out": centred(splits[16], (MI, MODEL_WIDTH), MI ** -0.5, 0.109375, ((0, 2),)),
        "ffn_gain": jnp.clip(jax.random.uniform(splits[17], (MODEL_WIDTH,), jnp.float32, 0.5, 1.5), 0.5, 1.5),
        "w_gate_up": centred(splits[18], (2, MODEL_WIDTH, FF), MODEL_WIDTH ** -0.5, 0.15625, ((2, 2),)),
        "w_down": centred(splits[19], (FF, MODEL_WIDTH), FF ** -0.5, 0.078125, ((0, 2),)),
    }


epsilon = 1e-05
floor_score = -1e+30

def rms_scale(block_values):
    return lax.rsqrt(lax.optimization_barrier(jnp.mean(block_values * block_values, axis=-1, keepdims=True)) + epsilon)

def reference(hidden, slot_request, cache_length, block_keep, stored_keys, stored_values, ssm_state, norm_gain, query_key_value_weight, w_attn_out, mamba_in, select_proj, step_proj, step_bias, decay_log, skip_gain, w_mamba_out, ffn_gain, w_gate_up, w_down):
    att_width = QUERY_HEADS * HEAD_SIZE
    key_value_width = KEY_HEADS * HEAD_SIZE
    query_group = QUERY_HEADS // KEY_HEADS
    scale = HEAD_SIZE ** (-0.5)
    hidden_f = hidden.astype(jnp.float32)
    normed = (hidden_f * rms_scale(hidden_f) * norm_gain).astype(jnp.bfloat16)
    qkv = jnp.dot(normed, query_key_value_weight, preferred_element_type=jnp.float32).astype(jnp.bfloat16)
    query_vector = qkv[:, :att_width]
    fresh_entry = qkv[:, att_width:]
    x_inner = jnp.dot(normed, mamba_in[0], preferred_element_type=jnp.float32)
    z_gate = jnp.dot(normed, mamba_in[1], preferred_element_type=jnp.float32)
    inner_act = jax.nn.silu(x_inner).astype(jnp.bfloat16)
    select_full = jnp.dot(inner_act, select_proj, preferred_element_type=jnp.float32)
    step_low = select_full[:, :RANK]
    in_gain = select_full[:, RANK:RANK + NS]
    out_gain = select_full[:, RANK + NS:]
    step_size = jax.nn.softplus(jnp.dot(step_low, step_proj.astype(jnp.float32), precision=lax.Precision.HIGHEST) + step_bias)
    rates = -jnp.exp(decay_log)
    decay = jnp.exp(step_size[:, None, :] * rates[None])
    inner_f = inner_act.astype(jnp.float32)
    new_state = decay * ssm_state + (step_size * inner_f)[:, None, :] * in_gain[:, :, None]
    ssm_out = lax.optimization_barrier(jnp.sum(out_gain[:, :, None] * new_state, axis=1)) + skip_gain * inner_f
    mamba_act = (ssm_out * jax.nn.silu(z_gate)).astype(jnp.bfloat16)

    def attend_one(items):
        query_line, key_matrix, value_matrix, length, keep_row, cache_entry = items
        query_grouped4 = query_line.astype(jnp.float32).reshape(KEY_HEADS, query_group, HEAD_SIZE)
        block_keys = key_matrix.astype(jnp.float32).reshape(REQUEST_BLOCKS, BLOCK_POSITIONS, KEY_HEADS, HEAD_SIZE)
        block_values = value_matrix.astype(jnp.float32).reshape(REQUEST_BLOCKS, BLOCK_POSITIONS, KEY_HEADS, HEAD_SIZE)
        scores = jnp.einsum('kgd,jpkd->jkgp', query_grouped4, block_keys, precision=lax.Precision.HIGHEST) * scale
        position = jnp.arange(REQUEST_BLOCKS, dtype=jnp.int32)[:, None] * BLOCK_POSITIONS + jnp.arange(BLOCK_POSITIONS, dtype=jnp.int32)[None, :]
        valid = (position < length) & (keep_row[:, None] == 1)
        valid4 = valid[:, None, None, :]
        masked = jnp.where(valid4, scores, floor_score)
        block_max = lax.optimization_barrier(jnp.max(masked, axis=-1))
        weights = jnp.where(valid4, jnp.exp(masked - block_max[..., None]), 0.0)
        block_sum = lax.optimization_barrier(jnp.sum(weights, axis=-1))
        rounded = lax.optimization_barrier(weights.astype(jnp.bfloat16))
        block_acc = jnp.einsum('jkgp,jpkd->jkgd', rounded.astype(jnp.float32), block_values, precision=lax.Precision.HIGHEST)
        fresh_key = cache_entry[:key_value_width].astype(jnp.float32).reshape(KEY_HEADS, HEAD_SIZE)
        fresh_value = cache_entry[key_value_width:].astype(jnp.float32).reshape(KEY_HEADS, 1, HEAD_SIZE)
        own_score = jnp.einsum('kgd,kd->kg', query_grouped4, fresh_key, precision=lax.Precision.HIGHEST) * scale
        top = jnp.maximum(lax.optimization_barrier(jnp.max(block_max, axis=0)), own_score)
        rescale = jnp.exp(block_max - top[None])
        own_weight = jnp.exp(own_score - top)
        total = lax.optimization_barrier(jnp.sum(block_sum * rescale, axis=0)) + own_weight
        accum = lax.optimization_barrier(jnp.sum(block_acc * rescale[..., None], axis=0)) + own_weight[..., None] * fresh_value
        return (accum / total[..., None]).reshape(att_width).astype(jnp.bfloat16)
    attended = lax.map(attend_one, (query_vector, stored_keys, stored_values, cache_length, block_keep, fresh_entry))
    branch = jnp.dot(attended, w_attn_out, preferred_element_type=jnp.float32) + jnp.dot(mamba_act, w_mamba_out, preferred_element_type=jnp.float32)
    resid = (hidden_f + 0.5 * branch).astype(jnp.bfloat16)
    resid_f = resid.astype(jnp.float32)
    ffn_in = (resid_f * rms_scale(resid_f) * ffn_gain).astype(jnp.bfloat16)
    gate = jnp.dot(ffn_in, w_gate_up[0], preferred_element_type=jnp.float32)
    upper = jnp.dot(ffn_in, w_gate_up[1], preferred_element_type=jnp.float32)
    ffn_hidden = (jax.nn.silu(gate) * upper).astype(jnp.bfloat16)
    final_rows = (resid_f + jnp.dot(ffn_hidden, w_down, preferred_element_type=jnp.float32)).astype(jnp.bfloat16)
    hidden_out = jnp.zeros_like(final_rows).at[slot_request].set(final_rows)
    return (hidden_out, fresh_entry, new_state)
```

```python
from functools import partial

import jax
import jax.numpy as jnp
from jax import lax
from jax.experimental import pallas as pl
from jax.experimental.pallas import tpu as pltpu
from jax.sharding import PartitionSpec as P

QUERY_HEADS = 25
HEAD_SIZE = 64
KEY_HEADS = 5
NS = 16
RANK = 100
BLOCK_POSITIONS = 128


epsilon = 1e-05
floor_score = -1e30

MESH = pl.DeviceIdType.MESH
VMEM_BYTES = 60 * 1024 * 1024
ROWS = 16
HEAD_ROWS = 32
STAT_LANES = 512


def rms_scale(block_values):
    return lax.rsqrt(jnp.mean(block_values * block_values, axis=-1, keepdims=True) + epsilon)


def silu(value):
    return value * jax.nn.sigmoid(value)


def bdot(left, right):
    return jnp.dot(left, right, preferred_element_type=jnp.float32)


def row_dot(row, weight):
    tall = jnp.broadcast_to(row, (ROWS, row.shape[1]))
    return bdot(tall, weight)[0:1]


def cuts_of(total, step):
    edges = list(range(0, total, step)) + [total]
    if len(edges) > 2 and edges[-1] - edges[-2] < step // 2:
        edges.pop(-2)
    return list(zip(edges[:-1], edges[1:]))


def own_part(value, index, count):
    width = value.shape[1] // count
    part = value[:, :width]
    for other in range(1, count):
        part = jnp.where(index == other, value[:, other * width : (other + 1) * width], part)
    return part


def send_all(buf, send_sem, recv_sem, stage, count):
    me = lax.axis_index("blk")
    copies = []
    for k in range(1, count):
        target = lax.rem(me + k, count)
        copy = pltpu.make_async_remote_copy(
            src_ref=buf.at[me],
            dst_ref=buf.at[me],
            send_sem=send_sem.at[stage, k],
            recv_sem=recv_sem.at[stage, me],
            device_id={"blk": target},
            device_id_type=MESH,
        )
        copy.start()
        copies.append(copy)
    return copies


def wait_all(copies, buf, send_sem, recv_sem, stage, count):
    me = lax.axis_index("blk")
    for k in range(1, count):
        source = lax.rem(me + k, count)
        pltpu.make_async_remote_copy(
            src_ref=buf.at[source],
            dst_ref=buf.at[source],
            send_sem=send_sem.at[stage, k],
            recv_sem=recv_sem.at[stage, source],
            device_id={"blk": source},
            device_id_type=MESH,
        ).wait_recv()
    for copy in copies:
        copy.wait_send()


def total_of(buf, count):
    result = buf[0]
    for k in range(1, count):
        result = result + buf[k]
    return result


def branch_kernel(
    count,
    hidden_ref,
    length_ref,
    keep_ref,
    state_ref,
    norm_ref,
    bias_ref,
    decay_ref,
    skip_ref,
    keys_hbm,
    values_hbm,
    qkv_hbm,
    attn_hbm,
    mamba_hbm,
    select_hbm,
    step_hbm,
    out_hbm,
    resid_ref,
    fresh_ref,
    new_state_ref,
    keys_ref,
    values_ref,
    qkv_w,
    attn_w,
    mamba_w,
    select_w,
    step_w,
    out_w,
    qkv_buf,
    sel_buf,
    stat_buf,
    mix_buf,
    load_sem,
    send_sem,
    recv_sem,
):
    me = lax.axis_index("blk")
    width = hidden_ref.shape[1]
    channels = state_ref.shape[2]
    positions = keys_ref.shape[0]
    key_width = KEY_HEADS * HEAD_SIZE
    group = QUERY_HEADS // KEY_HEADS
    att_width = QUERY_HEADS * HEAD_SIZE
    loads = []

    def load(source, target):
        copy = pltpu.make_async_copy(source, target, load_sem.at[len(loads)])
        copy.start()
        loads.append(copy)
        return copy

    feat_cuts = cuts_of(width, 512)
    load_qkv = load(qkv_hbm, qkv_w)
    load_x = [load(mamba_hbm.at[0, a:b], mamba_w.at[0, a:b]) for a, b in feat_cuts]
    load_select = load(select_hbm, select_w)
    load_keys = load(keys_hbm.at[0], keys_ref)
    load_values = load(values_hbm.at[0], values_ref)
    load_z = [load(mamba_hbm.at[1, a:b], mamba_w.at[1, a:b]) for a, b in feat_cuts]
    load_step = load(step_hbm, step_w)
    chan_cuts = cuts_of(channels, 512)
    load_out = [load(out_hbm.at[a:b], out_w.at[a:b]) for a, b in chan_cuts]
    load_attn = load(attn_hbm, attn_w)

    barrier = pltpu.get_barrier_semaphore()
    for k in range(1, count):
        pl.semaphore_signal(
            barrier, inc=1, device_id={"blk": lax.rem(me + k, count)}, device_id_type=MESH
        )
    pl.semaphore_wait(barrier, count - 1)

    hidden_f = hidden_ref[...].astype(jnp.float32)
    normed_f = hidden_f * rms_scale(hidden_f) * norm_ref[...].reshape(1, width)
    own_feat = own_part(normed_f, me, count).astype(jnp.bfloat16)
    normed = normed_f.astype(jnp.bfloat16)

    load_qkv.wait()
    qkv_buf[me] = row_dot(own_feat, qkv_w[...])
    sent_qkv = send_all(qkv_buf, send_sem, recv_sem, 0, count)

    def feature_dot(which, waits):
        result = jnp.zeros((1, channels), jnp.float32)
        for (a, b), wait in zip(feat_cuts, waits):
            wait.wait()
            result = result + row_dot(normed[:, a:b], mamba_w[which, a:b])
        return result

    inner_act = silu(feature_dot(0, load_x)).astype(jnp.bfloat16)
    inner_f = inner_act.astype(jnp.float32)
    load_select.wait()
    sel_buf[me] = row_dot(inner_act, select_w[...])
    sent_sel = send_all(sel_buf, send_sem, recv_sem, 1, count)

    wait_all(sent_qkv, qkv_buf, send_sem, recv_sem, 0, count)
    qkv_f = total_of(qkv_buf, count).astype(jnp.bfloat16).astype(jnp.float32)
    fresh_ref[...] = qkv_f[:, att_width:].astype(jnp.bfloat16)
    query = qkv_f[:, :att_width]
    new_key = qkv_f[:, att_width : att_width + key_width]
    new_value = qkv_f[:, att_width + key_width :]

    def owner_column(flat):
        head_group = jnp.zeros_like(flat)
        for g in range(1, KEY_HEADS):
            head_group = head_group + (flat >= g * group * HEAD_SIZE).astype(jnp.int32)
        return head_group * HEAD_SIZE + (flat & (HEAD_SIZE - 1))

    flat_rows = lax.broadcasted_iota(jnp.int32, (att_width, key_width), 0)
    flat_cols = lax.broadcasted_iota(jnp.int32, (att_width, key_width), 1)
    spread = (owner_column(flat_rows) == flat_cols).astype(jnp.float32).astype(jnp.bfloat16)
    head_of = lax.broadcasted_iota(jnp.int32, (HEAD_ROWS, att_width), 0)
    head_lane = lax.broadcasted_iota(jnp.int32, (HEAD_ROWS, att_width), 1)
    query_rows = jnp.where(head_of == (head_lane >> 6), jnp.broadcast_to(query, head_of.shape), 0.0)
    query_f = bdot(query_rows.astype(jnp.bfloat16), spread)
    query_bf = query_f.astype(jnp.bfloat16)

    scale = HEAD_SIZE ** (-0.5)
    load_keys.wait()
    scores = (
        lax.dot_general(
            query_bf, keys_ref[...], (((1,), (1,)), ((), ())), preferred_element_type=jnp.float32
        )
        * scale
    )
    lane = lax.broadcasted_iota(jnp.int32, (1, positions), 1)
    kept = jnp.zeros((1, positions), jnp.int32)
    for j in range(positions // BLOCK_POSITIONS):
        kept = jnp.where((lane >> 7) == j, keep_ref[0, j], kept)
    limit = length_ref[0] - me * positions
    live = jnp.where(lane < limit, kept, 0) == 1
    live = jnp.broadcast_to(live, scores.shape)
    masked = jnp.where(live, scores, floor_score)
    local_max = jnp.max(masked, axis=-1, keepdims=True)
    weights = jnp.where(live, jnp.exp(masked - local_max), 0.0)
    local_sum = jnp.sum(weights, axis=-1, keepdims=True)
    load_values.wait()
    stat_buf[me, :, :key_width] = bdot(weights.astype(jnp.bfloat16), values_ref[...])
    stat_lane = lax.broadcasted_iota(jnp.int32, (HEAD_ROWS, 128), 1)
    stat_buf[me, :, STAT_LANES - 128 :] = jnp.where(stat_lane < 64, local_max, local_sum)
    sent_stat = send_all(stat_buf, send_sem, recv_sem, 2, count)

    z_act = silu(feature_dot(1, load_z))

    wait_all(sent_sel, sel_buf, send_sem, recv_sem, 1, count)
    select_full = total_of(sel_buf, count)
    low = select_full[:, :RANK]
    low_a = low.astype(jnp.bfloat16).astype(jnp.float32)
    low_b = (low - low_a).astype(jnp.bfloat16).astype(jnp.float32)
    low_c = low - low_a - low_b
    term = lax.broadcasted_iota(jnp.int32, (ROWS, RANK), 0)
    terms = jnp.where(term == 0, low_a, jnp.where(term == 1, low_b, jnp.where(term == 2, low_c, 0.0)))
    load_step.wait()
    step_rows = bdot(terms.astype(jnp.bfloat16), step_w[...])
    raw = step_rows[0:1] + step_rows[1:2] + step_rows[2:3] + bias_ref[...].reshape(1, channels)
    step_size = jnp.maximum(raw, 0.0) + jnp.log1p(jnp.exp(-jnp.abs(raw)))

    gain_rows = lax.broadcasted_iota(jnp.int32, (NS, RANK + 2 * NS), 0)
    gain_lane = lax.broadcasted_iota(jnp.int32, (NS, RANK + 2 * NS), 1)
    select_rows = jnp.broadcast_to(select_full, gain_rows.shape)
    in_gain = jnp.sum(
        jnp.where(gain_lane == gain_rows + RANK, select_rows, 0.0), axis=1, keepdims=True
    )
    out_gain = jnp.sum(
        jnp.where(gain_lane == gain_rows + (RANK + NS), select_rows, 0.0), axis=1, keepdims=True
    )
    decay = jnp.exp(-step_size * jnp.exp(decay_ref[...]))
    new_state = decay * state_ref[0] + (step_size * inner_f) * in_gain
    new_state_ref[0] = new_state
    ssm_out = jnp.sum(out_gain * new_state, axis=0, keepdims=True)
    ssm_out = ssm_out + skip_ref[...].reshape(1, channels) * inner_f
    mamba_act = (ssm_out * z_act).astype(jnp.bfloat16)
    mix = jnp.zeros((1, width), jnp.float32)
    for (a, b), wait in zip(chan_cuts, load_out):
        wait.wait()
        mix = mix + row_dot(mamba_act[:, a:b], out_w[a:b])

    wait_all(sent_stat, stat_buf, send_sem, recv_sem, 2, count)
    own_score = jnp.sum(query_f * new_key, axis=-1, keepdims=True) * scale
    highest = own_score
    for k in range(count):
        highest = jnp.maximum(highest, stat_buf[k, :, STAT_LANES - 128 : STAT_LANES - 127])
    total = jnp.zeros_like(own_score)
    accum = jnp.zeros((HEAD_ROWS, key_width), jnp.float32)
    for k in range(count):
        factor = jnp.exp(stat_buf[k, :, STAT_LANES - 128 : STAT_LANES - 127] - highest)
        total = total + stat_buf[k, :, STAT_LANES - 64 : STAT_LANES - 63] * factor
        accum = accum + stat_buf[k, :, :key_width] * factor
    own_weight = jnp.exp(own_score - highest)
    total = total + own_weight
    accum = accum + own_weight * new_value
    attended = accum / total
    att_rows = lax.broadcasted_iota(jnp.int32, attended.shape, 0)
    att_cols = lax.broadcasted_iota(jnp.int32, attended.shape, 1) >> 6
    att_group = jnp.zeros_like(att_rows)
    for g in range(1, KEY_HEADS):
        att_group = att_group + (att_rows >= g * group).astype(jnp.int32)
    attended = jnp.where(att_group == att_cols, attended, 0.0).astype(jnp.bfloat16)
    part = att_width // count
    gather_rows = lax.broadcasted_iota(jnp.int32, (key_width, part), 0)
    gather_cols = lax.broadcasted_iota(jnp.int32, (key_width, part), 1) + me * part
    gather = (owner_column(gather_cols) == gather_rows).astype(jnp.float32).astype(jnp.bfloat16)
    att_flat = bdot(attended, gather)
    flat_head = lax.broadcasted_iota(jnp.int32, (HEAD_ROWS, part), 0)
    flat_lane = (lax.broadcasted_iota(jnp.int32, (HEAD_ROWS, part), 1) + me * part) >> 6
    own_att = jnp.sum(jnp.where(flat_head == flat_lane, att_flat, 0.0), axis=0, keepdims=True)
    load_attn.wait()
    mix = mix + row_dot(own_att.astype(jnp.bfloat16), attn_w[...])
    mix_buf[me] = 0.5 * mix
    sent_mix = send_all(mix_buf, send_sem, recv_sem, 3, count)
    wait_all(sent_mix, mix_buf, send_sem, recv_sem, 3, count)
    resid_ref[...] = (hidden_f + total_of(mix_buf, count)).astype(jnp.bfloat16)


def mix_branches(
    hidden, cache_length, block_keep, stored_keys, stored_values, ssm_state, norm_gain,
    query_key_value_weight, w_attn_out, mamba_in, select_proj, step_proj, step_bias, decay_log,
    skip_gain, w_mamba_out,
):
    count = lax.axis_size("blk")
    width = hidden.shape[1]
    channels = ssm_state.shape[2]
    qkv_width = query_key_value_weight.shape[1]
    vmem = pl.BlockSpec(memory_space=pltpu.VMEM)
    smem = pl.BlockSpec(memory_space=pltpu.SMEM)
    hbm = pl.BlockSpec(memory_space=pl.ANY)
    big = (query_key_value_weight, w_attn_out, mamba_in, select_proj, step_proj, w_mamba_out)
    return pl.pallas_call(
        partial(branch_kernel, count),
        out_shape=(
            jax.ShapeDtypeStruct(hidden.shape, jnp.bfloat16),
            jax.ShapeDtypeStruct((1, 2 * KEY_HEADS * HEAD_SIZE), jnp.bfloat16),
            jax.ShapeDtypeStruct(ssm_state.shape, jnp.float32),
        ),
        in_specs=[vmem, smem, smem, vmem, vmem, vmem, vmem, vmem] + [hbm] * 8,
        out_specs=(vmem, vmem, vmem),
        scratch_shapes=[
            pltpu.VMEM(stored_keys.shape[1:], jnp.bfloat16),
            pltpu.VMEM(stored_values.shape[1:], jnp.bfloat16),
        ]
        + [pltpu.VMEM(w.shape, w.dtype) for w in big]
        + [
            pltpu.VMEM((count, 1, qkv_width), jnp.float32),
            pltpu.VMEM((count, 1, select_proj.shape[1]), jnp.float32),
            pltpu.VMEM((count, HEAD_ROWS, STAT_LANES), jnp.float32),
            pltpu.VMEM((count, 1, width), jnp.float32),
            pltpu.SemaphoreType.DMA((32,)),
            pltpu.SemaphoreType.DMA((4, count)),
            pltpu.SemaphoreType.DMA((4, count)),
        ],
        compiler_params=pltpu.CompilerParams(
            collective_id=0, has_side_effects=True, vmem_limit_bytes=VMEM_BYTES
        ),
    )(
        hidden, cache_length, block_keep, ssm_state, norm_gain, step_bias, decay_log, skip_gain,
        stored_keys, stored_values, *big,
    )


def ffn_kernel(
    groups, count, tile, hidden_units,
    resid_ref, gain_ref, slot_ref, gate_up_ref, down_ref,
    out_ref,
    row_buf, rows_ref, part_buf, take_buf, row_send, row_recv, part_send, part_recv,
):
    devices = groups * count
    grp = lax.axis_index("req")
    blk = lax.axis_index("blk")
    me = grp * count + blk
    width = resid_ref.shape[1]
    half = width // count

    barrier = pltpu.get_barrier_semaphore()

    @pl.loop(1, devices)
    def _(k):
        target = lax.rem(me + k, devices)
        pl.semaphore_signal(
            barrier,
            inc=1,
            device_id=(target // count, lax.rem(target, count)),
            device_id_type=MESH,
        )

    row_buf[grp] = resid_ref[...].astype(jnp.float32)
    pl.semaphore_wait(barrier, devices - 1)

    def row_copy(k, slot, peer):
        return pltpu.make_async_remote_copy(
            src_ref=row_buf.at[slot],
            dst_ref=row_buf.at[slot],
            send_sem=row_send.at[k],
            recv_sem=row_recv.at[slot],
            device_id=(peer, blk),
            device_id_type=MESH,
        )

    @pl.loop(1, groups)
    def _(k):
        row_copy(k, grp, lax.rem(grp + k, groups)).start()

    @pl.loop(1, groups)
    def _(k):
        peer = lax.rem(grp + k, groups)
        row_copy(k, peer, peer).wait_recv()

    for r in range(groups):
        rows_ref[r : r + 1, :] = row_buf[r]
    resid_f = rows_ref[...]
    ffn_in = (resid_f * rms_scale(resid_f) * gain_ref[...].reshape(1, width)).astype(jnp.bfloat16)
    gate = bdot(ffn_in, gate_up_ref[0])
    upper = bdot(ffn_in, gate_up_ref[1])
    unit = grp * tile + lax.broadcasted_iota(jnp.int32, (groups, tile), 1)
    ffn_hidden = jnp.where(unit < hidden_units, silu(gate) * upper, 0.0).astype(jnp.bfloat16)
    lane = lax.broadcasted_iota(jnp.int32, (groups, groups), 1)
    slots = jnp.zeros((groups, groups), jnp.int32)
    for s in range(groups):
        slots = jnp.where(lane == s, slot_ref[s], slots)
    request = lax.broadcasted_iota(jnp.int32, (groups, groups), 0)
    picker = (slots == request).astype(jnp.float32).astype(jnp.bfloat16)
    placed = bdot(picker, ffn_hidden).astype(jnp.bfloat16)
    weight_unit = grp * tile + lax.broadcasted_iota(jnp.int32, (tile, width), 0)
    down = jnp.where(weight_unit < hidden_units, down_ref[...].astype(jnp.float32), 0.0)
    terms = bdot(placed, down.astype(jnp.bfloat16))
    for b in range(count):
        piece = terms[:, b * half : (b + 1) * half]
        for r in range(groups):
            part_buf[b, r] = piece[r : r + 1]

    def part_copy(k, slot, peer):
        return pltpu.make_async_remote_copy(
            src_ref=part_buf.at[lax.rem(peer, count), peer // count],
            dst_ref=take_buf.at[slot],
            send_sem=part_send.at[k],
            recv_sem=part_recv.at[slot],
            device_id=(peer // count, lax.rem(peer, count)),
            device_id_type=MESH,
        )

    @pl.loop(1, devices)
    def _(k):
        part_copy(k, me, lax.rem(me + k, devices)).start()

    take_buf[me] = part_buf[blk, grp]
    moved = bdot(picker, resid_f.astype(jnp.bfloat16))
    rows_ref[...] = moved
    own_row = own_part(rows_ref[pl.ds(grp, 1), :], blk, count)

    @pl.loop(1, devices)
    def _(k):
        peer = lax.rem(me + k, devices)
        part_copy(k, peer, peer).wait_recv()

    out_ref[...] = (own_row + jnp.sum(take_buf[...], axis=0)).astype(jnp.bfloat16)

    @pl.loop(1, groups)
    def _(k):
        row_copy(k, grp, lax.rem(grp + k, groups)).wait_send()

    @pl.loop(1, devices)
    def _(k):
        part_copy(k, me, lax.rem(me + k, devices)).wait_send()


def ffn_spread(resid, ffn_gain, slot_request, w_gate_up, w_down):
    groups = lax.axis_size("req")
    count = lax.axis_size("blk")
    width = resid.shape[1]
    units = w_down.shape[0]
    tile = -(-units // (groups * 128)) * 128
    last = -(-units // tile) - 1
    vmem = pl.BlockSpec(memory_space=pltpu.VMEM)
    return pl.pallas_call(
        partial(ffn_kernel, groups, count, tile, units),
        grid=(1,),
        out_shape=jax.ShapeDtypeStruct((1, width // count), jnp.bfloat16),
        in_specs=[
            vmem,
            vmem,
            pl.BlockSpec(memory_space=pltpu.SMEM),
            pl.BlockSpec(
                (2, width, tile), lambda i: (0, 0, jnp.minimum(lax.axis_index("req"), last))
            ),
            pl.BlockSpec((tile, width), lambda i: (jnp.minimum(lax.axis_index("req"), last), 0)),
        ],
        out_specs=vmem,
        scratch_shapes=[
            pltpu.VMEM((groups, 1, width), jnp.float32),
            pltpu.VMEM((groups, width), jnp.float32),
            pltpu.VMEM((count, groups, 1, width // count), jnp.float32),
            pltpu.VMEM((groups * count, 1, width // count), jnp.float32),
            pltpu.SemaphoreType.DMA((groups,)),
            pltpu.SemaphoreType.DMA((groups,)),
            pltpu.SemaphoreType.DMA((groups * count,)),
            pltpu.SemaphoreType.DMA((groups * count,)),
        ],
        compiler_params=pltpu.CompilerParams(
            collective_id=1, has_side_effects=True, vmem_limit_bytes=VMEM_BYTES
        ),
    )(resid, ffn_gain, slot_request, w_gate_up, w_down)


def ffn_plain(resid, ffn_gain, slot_request, w_gate_up, w_down):
    blk_index = lax.axis_index("blk")
    grp_index = lax.axis_index("req")
    resid_f = resid.astype(jnp.float32)
    ffn_in = (resid_f * rms_scale(resid_f) * ffn_gain).astype(jnp.bfloat16)
    ffn_hidden = (silu(bdot(ffn_in, w_gate_up[0])) * bdot(ffn_in, w_gate_up[1])).astype(
        jnp.bfloat16
    )
    ffn_out = lax.psum(bdot(ffn_hidden, w_down), "blk")
    final_rows = (resid_f + ffn_out).astype(jnp.bfloat16)
    every_row = lax.all_gather(final_rows, "req", axis=0, tiled=True)
    part = resid.shape[1] // lax.axis_size("blk")
    columns = lax.dynamic_slice_in_dim(every_row, blk_index * part, part, 1)
    picker = (slot_request[None, :] == grp_index).astype(jnp.bfloat16)
    return bdot(picker, columns).astype(jnp.bfloat16)


def per_device(
    hidden,
    slot_request,
    cache_length,
    block_keep,
    stored_keys,
    stored_values,
    ssm_state,
    norm_gain,
    query_key_value_weight,
    w_attn_out,
    mamba_in,
    select_proj,
    step_proj,
    step_bias,
    decay_log,
    skip_gain,
    w_mamba_out,
    ffn_gain,
    w_gate_up,
    w_down,
):
    resid, fresh_entry, new_state = mix_branches(
        hidden, cache_length, block_keep, stored_keys, stored_values, ssm_state, norm_gain,
        query_key_value_weight, w_attn_out, mamba_in, select_proj, step_proj, step_bias,
        decay_log, skip_gain, w_mamba_out,
    )
    ffn = ffn_spread if lax.axis_size("req") <= 16 else ffn_plain
    hidden_out = ffn(resid, ffn_gain, slot_request, w_gate_up, w_down)
    return (hidden_out, fresh_entry, new_state)


def solution(mesh):
    return jax.shard_map(
        per_device,
        mesh=mesh,
        in_specs=(
            P("req", None),
            P(),
            P("req"),
            P("req", "blk"),
            P("req", "blk", None),
            P("req", "blk", None),
            P("req", None, "blk"),
            P(),
            P("blk", None),
            P("blk", None),
            P(None, None, "blk"),
            P("blk", None),
            P(None, "blk"),
            P("blk"),
            P(None, "blk"),
            P("blk"),
            P("blk", None),
            P(),
            P(None, None, "blk"),
            P("blk", None),
        ),
        out_specs=(P("req", "blk"), P("req", None), P("req", None, "blk")),
        check_vma=False,
    )
```

```python
from functools import partial

import jax
import jax.numpy as jnp
from jax import lax
from jax.experimental import pallas as pl
from jax.experimental.pallas import tpu as pltpu
from jax.sharding import PartitionSpec as P

QUERY_HEADS = 25
HEAD_SIZE = 64
KEY_HEADS = 5
NS = 16
RANK = 100
BLOCK_POSITIONS = 128


epsilon = 1e-05
floor_score = -1e30

MESH = pl.DeviceIdType.MESH
VMEM_BYTES = 60 * 1024 * 1024
ROWS = 16
HEAD_ROWS = 32
STAT_LANES = 512


def rms_scale(block_values):
    return lax.rsqrt(jnp.mean(block_values * block_values, axis=-1, keepdims=True) + epsilon)


def silu(value):
    return value * jax.nn.sigmoid(value)


def bdot(left, right):
    return jnp.dot(left, right, preferred_element_type=jnp.float32)


def bdot_t(left, right):
    return lax.dot_general(
        left, right, (((1,), (1,)), ((), ())), preferred_element_type=jnp.float32
    )


def row_dot(row, weight):
    tall = jnp.broadcast_to(row, (ROWS, row.shape[1]))
    return bdot(tall, weight)[0:1]


def cuts_of(total, step):
    edges = list(range(0, total, step)) + [total]
    if len(edges) > 2 and edges[-1] - edges[-2] < step // 2:
        edges.pop(-2)
    return list(zip(edges[:-1], edges[1:]))


def own_part(value, index, count):
    width = value.shape[1] // count
    part = value[:, :width]
    for other in range(1, count):
        part = jnp.where(index == other, value[:, other * width : (other + 1) * width], part)
    return part


def send_all(buf, send_sem, recv_sem, stage, count):
    me = lax.axis_index("blk")
    copies = []
    for k in range(1, count):
        target = lax.rem(me + k, count)
        copy = pltpu.make_async_remote_copy(
            src_ref=buf.at[me],
            dst_ref=buf.at[me],
            send_sem=send_sem.at[stage, k],
            recv_sem=recv_sem.at[stage, me],
            device_id={"blk": target},
            device_id_type=MESH,
        )
        copy.start()
        copies.append(copy)
    return copies


def wait_all(copies, buf, send_sem, recv_sem, stage, count):
    me = lax.axis_index("blk")
    for k in range(1, count):
        source = lax.rem(me + k, count)
        pltpu.make_async_remote_copy(
            src_ref=buf.at[source],
            dst_ref=buf.at[source],
            send_sem=send_sem.at[stage, k],
            recv_sem=recv_sem.at[stage, source],
            device_id={"blk": source},
            device_id_type=MESH,
        ).wait_recv()
    for copy in copies:
        copy.wait_send()


def total_of(buf, count):
    result = buf[0]
    for k in range(1, count):
        result = result + buf[k]
    return result


def branch_kernel(
    count,
    hidden_ref,
    length_ref,
    keep_ref,
    state_ref,
    norm_ref,
    bias_ref,
    decay_ref,
    skip_ref,
    keys_hbm,
    values_hbm,
    qkv_hbm,
    attn_hbm,
    mamba_hbm,
    select_hbm,
    step_hbm,
    out_hbm,
    resid_ref,
    fresh_ref,
    new_state_ref,
    keys_ref,
    values_ref,
    qkv_w,
    attn_w,
    mamba_w,
    select_w,
    step_w,
    out_w,
    qkv_buf,
    sel_buf,
    stat_buf,
    mix_buf,
    load_sem,
    send_sem,
    recv_sem,
):
    me = lax.axis_index("blk")
    width = hidden_ref.shape[1]
    channels = state_ref.shape[2]
    positions = keys_ref.shape[1]
    key_width = KEY_HEADS * HEAD_SIZE
    group = QUERY_HEADS // KEY_HEADS
    att_width = QUERY_HEADS * HEAD_SIZE
    loads = []

    def load(source, target):
        copy = pltpu.make_async_copy(source, target, load_sem.at[len(loads)])
        copy.start()
        loads.append(copy)
        return copy

    feat_cuts = cuts_of(width, 512)
    load_qkv = load(qkv_hbm, qkv_w)
    load_x = [load(mamba_hbm.at[0, a:b], mamba_w.at[0, a:b]) for a, b in feat_cuts]
    load_select = load(select_hbm, select_w)
    load_keys = load(keys_hbm.at[0], keys_ref)
    load_values = load(values_hbm.at[0], values_ref)
    load_z = [load(mamba_hbm.at[1, a:b], mamba_w.at[1, a:b]) for a, b in feat_cuts]
    load_step = load(step_hbm, step_w)
    chan_cuts = cuts_of(channels, 512)
    load_out = [load(out_hbm.at[a:b], out_w.at[a:b]) for a, b in chan_cuts]
    load_attn = load(attn_hbm, attn_w)

    barrier = pltpu.get_barrier_semaphore()
    for k in range(1, count):
        pl.semaphore_signal(
            barrier, inc=1, device_id={"blk": lax.rem(me + k, count)}, device_id_type=MESH
        )
    pl.semaphore_wait(barrier, count - 1)

    hidden_f = hidden_ref[...].astype(jnp.float32)
    normed_f = hidden_f * rms_scale(hidden_f) * norm_ref[...].reshape(1, width)
    own_feat = own_part(normed_f, me, count).astype(jnp.bfloat16)
    normed = normed_f.astype(jnp.bfloat16)

    load_qkv.wait()
    qkv_buf[me] = row_dot(own_feat, qkv_w[...])
    sent_qkv = send_all(qkv_buf, send_sem, recv_sem, 0, count)

    def feature_dot(which, waits):
        result = jnp.zeros((1, channels), jnp.float32)
        for (a, b), wait in zip(feat_cuts, waits):
            wait.wait()
            result = result + row_dot(normed[:, a:b], mamba_w[which, a:b])
        return result

    inner_act = silu(feature_dot(0, load_x)).astype(jnp.bfloat16)
    inner_f = inner_act.astype(jnp.float32)
    load_select.wait()
    sel_buf[me] = bdot_t(jnp.broadcast_to(inner_act, (ROWS, channels)), select_w[...])[0:1]
    sent_sel = send_all(sel_buf, send_sem, recv_sem, 1, count)

    wait_all(sent_qkv, qkv_buf, send_sem, recv_sem, 0, count)
    qkv_f = total_of(qkv_buf, count).astype(jnp.bfloat16).astype(jnp.float32)
    fresh_ref[...] = qkv_f[:, att_width:].astype(jnp.bfloat16)
    query = qkv_f[:, :att_width]
    new_key = qkv_f[:, att_width : att_width + key_width]
    new_value = qkv_f[:, att_width + key_width :]

    def owner_column(flat):
        head_group = jnp.zeros_like(flat)
        for g in range(1, KEY_HEADS):
            head_group = head_group + (flat >= g * group * HEAD_SIZE).astype(jnp.int32)
        return head_group * HEAD_SIZE + (flat & (HEAD_SIZE - 1))

    flat_rows = lax.broadcasted_iota(jnp.int32, (att_width, key_width), 0)
    flat_cols = lax.broadcasted_iota(jnp.int32, (att_width, key_width), 1)
    spread = (owner_column(flat_rows) == flat_cols).astype(jnp.float32).astype(jnp.bfloat16)
    head_of = lax.broadcasted_iota(jnp.int32, (HEAD_ROWS, att_width), 0)
    head_lane = lax.broadcasted_iota(jnp.int32, (HEAD_ROWS, att_width), 1)
    query_rows = jnp.where(head_of == (head_lane >> 6), jnp.broadcast_to(query, head_of.shape), 0.0)
    query_f = bdot(query_rows.astype(jnp.bfloat16), spread)
    query_bf = query_f.astype(jnp.bfloat16)

    scale = HEAD_SIZE ** (-0.5)
    load_keys.wait()
    scores = bdot(query_bf, keys_ref[...]) * scale
    lane = lax.broadcasted_iota(jnp.int32, (1, positions), 1)
    kept = jnp.zeros((1, positions), jnp.int32)
    for j in range(positions // BLOCK_POSITIONS):
        kept = jnp.where((lane >> 7) == j, keep_ref[0, j], kept)
    limit = length_ref[0] - me * positions
    live = jnp.where(lane < limit, kept, 0) == 1
    live = jnp.broadcast_to(live, scores.shape)
    masked = jnp.where(live, scores, floor_score)
    local_max = jnp.max(masked, axis=-1, keepdims=True)
    weights = jnp.where(live, jnp.exp(masked - local_max), 0.0)
    local_sum = jnp.sum(weights, axis=-1, keepdims=True)
    load_values.wait()
    stat_buf[me, :, :key_width] = bdot_t(weights.astype(jnp.bfloat16), values_ref[...])
    stat_lane = lax.broadcasted_iota(jnp.int32, (HEAD_ROWS, 128), 1)
    stat_buf[me, :, STAT_LANES - 128 :] = jnp.where(stat_lane < 64, local_max, local_sum)
    sent_stat = send_all(stat_buf, send_sem, recv_sem, 2, count)

    z_act = silu(feature_dot(1, load_z))

    wait_all(sent_sel, sel_buf, send_sem, recv_sem, 1, count)
    select_full = total_of(sel_buf, count)
    low = select_full[:, :RANK]
    low_a = low.astype(jnp.bfloat16).astype(jnp.float32)
    low_b = (low - low_a).astype(jnp.bfloat16).astype(jnp.float32)
    low_c = low - low_a - low_b
    term = lax.broadcasted_iota(jnp.int32, (ROWS, RANK), 0)
    terms = jnp.where(term == 0, low_a, jnp.where(term == 1, low_b, jnp.where(term == 2, low_c, 0.0)))
    load_step.wait()
    step_rows = bdot(terms.astype(jnp.bfloat16), step_w[...])
    raw = step_rows[0:1] + step_rows[1:2] + step_rows[2:3] + bias_ref[...].reshape(1, channels)
    step_size = jnp.maximum(raw, 0.0) + jnp.log1p(jnp.exp(-jnp.abs(raw)))

    gain_rows = lax.broadcasted_iota(jnp.int32, (NS, RANK + 2 * NS), 0)
    gain_lane = lax.broadcasted_iota(jnp.int32, (NS, RANK + 2 * NS), 1)
    select_rows = jnp.broadcast_to(select_full, gain_rows.shape)
    in_gain = jnp.sum(
        jnp.where(gain_lane == gain_rows + RANK, select_rows, 0.0), axis=1, keepdims=True
    )
    out_gain = jnp.sum(
        jnp.where(gain_lane == gain_rows + (RANK + NS), select_rows, 0.0), axis=1, keepdims=True
    )
    decay = jnp.exp(-step_size * jnp.exp(decay_ref[...]))
    new_state = decay * state_ref[0] + (step_size * inner_f) * in_gain
    new_state_ref[0] = new_state
    ssm_out = jnp.sum(out_gain * new_state, axis=0, keepdims=True)
    ssm_out = ssm_out + skip_ref[...].reshape(1, channels) * inner_f
    mamba_act = (ssm_out * z_act).astype(jnp.bfloat16)
    mix = jnp.zeros((1, width), jnp.float32)
    for (a, b), wait in zip(chan_cuts, load_out):
        wait.wait()
        mix = mix + row_dot(mamba_act[:, a:b], out_w[a:b])

    wait_all(sent_stat, stat_buf, send_sem, recv_sem, 2, count)
    own_score = jnp.sum(query_f * new_key, axis=-1, keepdims=True) * scale
    highest = own_score
    for k in range(count):
        highest = jnp.maximum(highest, stat_buf[k, :, STAT_LANES - 128 : STAT_LANES - 127])
    total = jnp.zeros_like(own_score)
    accum = jnp.zeros((HEAD_ROWS, key_width), jnp.float32)
    for k in range(count):
        factor = jnp.exp(stat_buf[k, :, STAT_LANES - 128 : STAT_LANES - 127] - highest)
        total = total + stat_buf[k, :, STAT_LANES - 64 : STAT_LANES - 63] * factor
        accum = accum + stat_buf[k, :, :key_width] * factor
    own_weight = jnp.exp(own_score - highest)
    total = total + own_weight
    accum = accum + own_weight * new_value
    attended = accum / total
    att_rows = lax.broadcasted_iota(jnp.int32, attended.shape, 0)
    att_cols = lax.broadcasted_iota(jnp.int32, attended.shape, 1) >> 6
    att_group = jnp.zeros_like(att_rows)
    for g in range(1, KEY_HEADS):
        att_group = att_group + (att_rows >= g * group).astype(jnp.int32)
    attended = jnp.where(att_group == att_cols, attended, 0.0).astype(jnp.bfloat16)
    part = att_width // count
    gather_rows = lax.broadcasted_iota(jnp.int32, (key_width, part), 0)
    gather_cols = lax.broadcasted_iota(jnp.int32, (key_width, part), 1) + me * part
    gather = (owner_column(gather_cols) == gather_rows).astype(jnp.float32).astype(jnp.bfloat16)
    att_flat = bdot(attended, gather)
    flat_head = lax.broadcasted_iota(jnp.int32, (HEAD_ROWS, part), 0)
    flat_lane = (lax.broadcasted_iota(jnp.int32, (HEAD_ROWS, part), 1) + me * part) >> 6
    own_att = jnp.sum(jnp.where(flat_head == flat_lane, att_flat, 0.0), axis=0, keepdims=True)
    load_attn.wait()
    mix = mix + row_dot(own_att.astype(jnp.bfloat16), attn_w[...])
    mix_buf[me] = 0.5 * mix
    sent_mix = send_all(mix_buf, send_sem, recv_sem, 3, count)
    wait_all(sent_mix, mix_buf, send_sem, recv_sem, 3, count)
    resid_ref[...] = (hidden_f + total_of(mix_buf, count)).astype(jnp.bfloat16)


def mix_branches(
    hidden, cache_length, block_keep, stored_keys, stored_values, ssm_state, norm_gain,
    query_key_value_weight, w_attn_out, mamba_in, select_proj, step_proj, step_bias, decay_log,
    skip_gain, w_mamba_out,
):
    count = lax.axis_size("blk")
    width = hidden.shape[1]
    channels = ssm_state.shape[2]
    qkv_width = query_key_value_weight.shape[1]
    vmem = pl.BlockSpec(memory_space=pltpu.VMEM)
    smem = pl.BlockSpec(memory_space=pltpu.SMEM)
    hbm = pl.BlockSpec(memory_space=pl.ANY)
    stored_keys, stored_values, select_proj = (
        jnp.swapaxes(a, -1, -2) for a in (stored_keys, stored_values, select_proj)
    )
    big = (query_key_value_weight, w_attn_out, mamba_in, select_proj, step_proj, w_mamba_out)
    return pl.pallas_call(
        partial(branch_kernel, count),
        out_shape=(
            jax.ShapeDtypeStruct(hidden.shape, jnp.bfloat16),
            jax.ShapeDtypeStruct((1, 2 * KEY_HEADS * HEAD_SIZE), jnp.bfloat16),
            jax.ShapeDtypeStruct(ssm_state.shape, jnp.float32),
        ),
        in_specs=[vmem, smem, smem, vmem, vmem, vmem, vmem, vmem] + [hbm] * 8,
        out_specs=(vmem, vmem, vmem),
        scratch_shapes=[
            pltpu.VMEM(stored_keys.shape[1:], jnp.bfloat16),
            pltpu.VMEM(stored_values.shape[1:], jnp.bfloat16),
        ]
        + [pltpu.VMEM(w.shape, w.dtype) for w in big]
        + [
            pltpu.VMEM((count, 1, qkv_width), jnp.float32),
            pltpu.VMEM((count, 1, select_proj.shape[0]), jnp.float32),
            pltpu.VMEM((count, HEAD_ROWS, STAT_LANES), jnp.float32),
            pltpu.VMEM((count, 1, width), jnp.float32),
            pltpu.SemaphoreType.DMA((32,)),
            pltpu.SemaphoreType.DMA((4, count)),
            pltpu.SemaphoreType.DMA((4, count)),
        ],
        compiler_params=pltpu.CompilerParams(
            collective_id=0, has_side_effects=True, vmem_limit_bytes=VMEM_BYTES
        ),
    )(
        hidden, cache_length, block_keep, ssm_state, norm_gain, step_bias, decay_log, skip_gain,
        stored_keys, stored_values, *big,
    )


def ffn_kernel(
    groups, count, tile, hidden_units,
    resid_ref, gain_ref, slot_ref, gate_up_ref, down_ref,
    out_ref,
    row_buf, rows_ref, part_buf, take_buf, row_send, row_recv, part_send, part_recv,
):
    devices = groups * count
    grp = lax.axis_index("req")
    blk = lax.axis_index("blk")
    me = grp * count + blk
    width = resid_ref.shape[1]
    half = width // count

    barrier = pltpu.get_barrier_semaphore()

    @pl.loop(1, devices)
    def _(k):
        target = lax.rem(me + k, devices)
        pl.semaphore_signal(
            barrier,
            inc=1,
            device_id=(target // count, lax.rem(target, count)),
            device_id_type=MESH,
        )

    row_buf[grp] = resid_ref[...].astype(jnp.float32)
    pl.semaphore_wait(barrier, devices - 1)

    def row_copy(k, slot, peer):
        return pltpu.make_async_remote_copy(
            src_ref=row_buf.at[slot],
            dst_ref=row_buf.at[slot],
            send_sem=row_send.at[k],
            recv_sem=row_recv.at[slot],
            device_id=(peer, blk),
            device_id_type=MESH,
        )

    @pl.loop(1, groups)
    def _(k):
        row_copy(k, grp, lax.rem(grp + k, groups)).start()

    @pl.loop(1, groups)
    def _(k):
        peer = lax.rem(grp + k, groups)
        row_copy(k, peer, peer).wait_recv()

    for r in range(groups):
        rows_ref[r : r + 1, :] = row_buf[r]
    resid_f = rows_ref[...]
    ffn_in = (resid_f * rms_scale(resid_f) * gain_ref[...].reshape(1, width)).astype(jnp.bfloat16)
    gate = bdot(ffn_in, gate_up_ref[0])
    upper = bdot(ffn_in, gate_up_ref[1])
    unit = grp * tile + lax.broadcasted_iota(jnp.int32, (groups, tile), 1)
    ffn_hidden = jnp.where(unit < hidden_units, silu(gate) * upper, 0.0).astype(jnp.bfloat16)
    lane = lax.broadcasted_iota(jnp.int32, (groups, groups), 1)
    slots = jnp.zeros((groups, groups), jnp.int32)
    for s in range(groups):
        slots = jnp.where(lane == s, slot_ref[s], slots)
    request = lax.broadcasted_iota(jnp.int32, (groups, groups), 0)
    picker = (slots == request).astype(jnp.float32).astype(jnp.bfloat16)
    placed = bdot(picker, ffn_hidden).astype(jnp.bfloat16)
    weight_unit = grp * tile + lax.broadcasted_iota(jnp.int32, (width, tile), 1)
    down = jnp.where(weight_unit < hidden_units, down_ref[...].astype(jnp.float32), 0.0)
    terms = bdot_t(placed, down.astype(jnp.bfloat16))
    for b in range(count):
        piece = terms[:, b * half : (b + 1) * half]
        for r in range(groups):
            part_buf[b, r] = piece[r : r + 1]

    def part_copy(k, slot, peer):
        return pltpu.make_async_remote_copy(
            src_ref=part_buf.at[lax.rem(peer, count), peer // count],
            dst_ref=take_buf.at[slot],
            send_sem=part_send.at[k],
            recv_sem=part_recv.at[slot],
            device_id=(peer // count, lax.rem(peer, count)),
            device_id_type=MESH,
        )

    @pl.loop(1, devices)
    def _(k):
        part_copy(k, me, lax.rem(me + k, devices)).start()

    take_buf[me] = part_buf[blk, grp]
    moved = bdot(picker, resid_f.astype(jnp.bfloat16))
    rows_ref[...] = moved
    own_row = own_part(rows_ref[pl.ds(grp, 1), :], blk, count)

    @pl.loop(1, devices)
    def _(k):
        peer = lax.rem(me + k, devices)
        part_copy(k, peer, peer).wait_recv()

    out_ref[...] = (own_row + jnp.sum(take_buf[...], axis=0)).astype(jnp.bfloat16)

    @pl.loop(1, groups)
    def _(k):
        row_copy(k, grp, lax.rem(grp + k, groups)).wait_send()

    @pl.loop(1, devices)
    def _(k):
        part_copy(k, me, lax.rem(me + k, devices)).wait_send()


def ffn_spread(resid, ffn_gain, slot_request, w_gate_up, w_down):
    groups = lax.axis_size("req")
    count = lax.axis_size("blk")
    width = resid.shape[1]
    units = w_down.shape[0]
    tile = -(-units // (groups * 128)) * 128
    last = -(-units // tile) - 1
    vmem = pl.BlockSpec(memory_space=pltpu.VMEM)
    return pl.pallas_call(
        partial(ffn_kernel, groups, count, tile, units),
        grid=(1,),
        out_shape=jax.ShapeDtypeStruct((1, width // count), jnp.bfloat16),
        in_specs=[
            vmem,
            vmem,
            pl.BlockSpec(memory_space=pltpu.SMEM),
            pl.BlockSpec(
                (2, width, tile), lambda i: (0, 0, jnp.minimum(lax.axis_index("req"), last))
            ),
            pl.BlockSpec((width, tile), lambda i: (0, jnp.minimum(lax.axis_index("req"), last))),
        ],
        out_specs=vmem,
        scratch_shapes=[
            pltpu.VMEM((groups, 1, width), jnp.float32),
            pltpu.VMEM((groups, width), jnp.float32),
            pltpu.VMEM((count, groups, 1, width // count), jnp.float32),
            pltpu.VMEM((groups * count, 1, width // count), jnp.float32),
            pltpu.SemaphoreType.DMA((groups,)),
            pltpu.SemaphoreType.DMA((groups,)),
            pltpu.SemaphoreType.DMA((groups * count,)),
            pltpu.SemaphoreType.DMA((groups * count,)),
        ],
        compiler_params=pltpu.CompilerParams(
            collective_id=1, has_side_effects=True, vmem_limit_bytes=VMEM_BYTES
        ),
    )(resid, ffn_gain, slot_request, w_gate_up, w_down.T)


def ffn_plain(resid, ffn_gain, slot_request, w_gate_up, w_down):
    blk_index = lax.axis_index("blk")
    grp_index = lax.axis_index("req")
    resid_f = resid.astype(jnp.float32)
    ffn_in = (resid_f * rms_scale(resid_f) * ffn_gain).astype(jnp.bfloat16)
    ffn_hidden = (silu(bdot(ffn_in, w_gate_up[0])) * bdot(ffn_in, w_gate_up[1])).astype(
        jnp.bfloat16
    )
    ffn_out = lax.psum(bdot(ffn_hidden, w_down), "blk")
    final_rows = (resid_f + ffn_out).astype(jnp.bfloat16)
    every_row = lax.all_gather(final_rows, "req", axis=0, tiled=True)
    part = resid.shape[1] // lax.axis_size("blk")
    columns = lax.dynamic_slice_in_dim(every_row, blk_index * part, part, 1)
    picker = (slot_request[None, :] == grp_index).astype(jnp.bfloat16)
    return bdot(picker, columns).astype(jnp.bfloat16)


def per_device(
    hidden,
    slot_request,
    cache_length,
    block_keep,
    stored_keys,
    stored_values,
    ssm_state,
    norm_gain,
    query_key_value_weight,
    w_attn_out,
    mamba_in,
    select_proj,
    step_proj,
    step_bias,
    decay_log,
    skip_gain,
    w_mamba_out,
    ffn_gain,
    w_gate_up,
    w_down,
):
    resid, fresh_entry, new_state = mix_branches(
        hidden, cache_length, block_keep, stored_keys, stored_values, ssm_state, norm_gain,
        query_key_value_weight, w_attn_out, mamba_in, select_proj, step_proj, step_bias,
        decay_log, skip_gain, w_mamba_out,
    )
    ffn = ffn_spread if lax.axis_size("req") <= 16 else ffn_plain
    hidden_out = ffn(resid, ffn_gain, slot_request, w_gate_up, w_down)
    return (hidden_out, fresh_entry, new_state)


def solution(mesh):
    return jax.shard_map(
        per_device,
        mesh=mesh,
        in_specs=(
            P("req", None),
            P(),
            P("req"),
            P("req", "blk"),
            P("req", "blk", None),
            P("req", "blk", None),
            P("req", None, "blk"),
            P(),
            P("blk", None),
            P("blk", None),
            P(None, None, "blk"),
            P("blk", None),
            P(None, "blk"),
            P("blk"),
            P(None, "blk"),
            P("blk"),
            P("blk", None),
            P(),
            P(None, None, "blk"),
            P("blk", None),
        ),
        out_specs=(P("req", "blk"), P("req", None), P("req", None, "blk")),
        check_vma=False,
    )
```

```python
from functools import partial

import jax
import jax.numpy as jnp
from jax import lax
from jax.experimental import pallas as pl
from jax.experimental.pallas import tpu as pltpu
from jax.sharding import PartitionSpec as P

QUERY_HEADS = 25
HEAD_SIZE = 64
KEY_HEADS = 5
NS = 16
RANK = 100
BLOCK_POSITIONS = 128


epsilon = 1e-05
floor_score = -1e30

MESH = pl.DeviceIdType.MESH
VMEM_BYTES = 60 * 1024 * 1024
ROWS = 16
HEAD_ROWS = 32
STAT_LANES = 512
LANES = 128


def rms_scale(block_values):
    return lax.rsqrt(jnp.mean(block_values * block_values, axis=-1, keepdims=True) + epsilon)


def silu(value):
    return value * jax.nn.sigmoid(value)


def bdot(left, right):
    return jnp.dot(left, right, preferred_element_type=jnp.float32)


def bdot_t(left, right):
    return lax.dot_general(
        left, right, (((1,), (1,)), ((), ())), preferred_element_type=jnp.float32
    )


def row_dot(row, weight):
    tall = jnp.broadcast_to(row, (ROWS, row.shape[1]))
    return bdot(tall, weight)[0:1]


def cuts_of(total, step):
    edges = list(range(0, total, step)) + [total]
    if len(edges) > 2 and edges[-1] - edges[-2] < step // 2:
        edges.pop(-2)
    return list(zip(edges[:-1], edges[1:]))


def own_part(value, index, count):
    width = value.shape[1] // count
    part = value[:, :width]
    for other in range(1, count):
        part = jnp.where(index == other, value[:, other * width : (other + 1) * width], part)
    return part


def send_all(buf, send_sem, recv_sem, stage, count):
    me = lax.axis_index("blk")
    copies = []
    for k in range(1, count):
        target = lax.rem(me + k, count)
        copy = pltpu.make_async_remote_copy(
            src_ref=buf.at[me],
            dst_ref=buf.at[me],
            send_sem=send_sem.at[stage, k],
            recv_sem=recv_sem.at[stage, me],
            device_id={"blk": target},
            device_id_type=MESH,
        )
        copy.start()
        copies.append(copy)
    return copies


def wait_all(copies, buf, send_sem, recv_sem, stage, count):
    me = lax.axis_index("blk")
    for k in range(1, count):
        source = lax.rem(me + k, count)
        pltpu.make_async_remote_copy(
            src_ref=buf.at[source],
            dst_ref=buf.at[source],
            send_sem=send_sem.at[stage, k],
            recv_sem=recv_sem.at[stage, source],
            device_id={"blk": source},
            device_id_type=MESH,
        ).wait_recv()
    for copy in copies:
        copy.wait_send()


def total_of(buf, count):
    result = buf[0]
    for k in range(1, count):
        result = result + buf[k]
    return result


def layer_kernel(
    count,
    groups,
    tile,
    spread_ffn,
    *refs,
):
    (
        hidden_ref, length_ref, keep_ref, state_ref, norm_ref, bias_ref, decay_ref, skip_ref,
        keys_hbm, values_hbm, qkv_hbm, attn_hbm, mamba_hbm, select_hbm, step_hbm, out_hbm,
    ) = refs[:16]
    refs = refs[16:]
    if spread_ffn:
        gain_ref, slot_ref, gate_up_hbm, down_hbm = refs[:4]
        refs = refs[4:]
    resid_ref, fresh_ref, new_state_ref = refs[:3]
    (
        keys_ref, values_ref, qkv_w, attn_w, mamba_w, select_w, step_w, out_w,
        qkv_buf, sel_buf, stat_buf, mix_buf, load_sem, send_sem, recv_sem,
    ) = refs[3:18]
    if spread_ffn:
        (
            gate_up_w, down_w, gate_up_tail, down_tail, row_buf, rows_ref, part_buf, take_buf,
            far_send, far_recv,
        ) = refs[18:]
    me = lax.axis_index("blk")
    width = hidden_ref.shape[1]
    channels = state_ref.shape[2]
    positions = keys_ref.shape[1]
    key_width = KEY_HEADS * HEAD_SIZE
    group = QUERY_HEADS // KEY_HEADS
    att_width = QUERY_HEADS * HEAD_SIZE
    loads = []

    def load(source, target):
        copy = pltpu.make_async_copy(source, target, load_sem.at[len(loads)])
        copy.start()
        loads.append(copy)
        return copy

    feat_cuts = cuts_of(width, 512)
    load_qkv = load(qkv_hbm, qkv_w)
    load_x = [load(mamba_hbm.at[0, a:b], mamba_w.at[0, a:b]) for a, b in feat_cuts]
    load_select = load(select_hbm, select_w)
    load_keys = load(keys_hbm.at[0], keys_ref)
    load_values = load(values_hbm.at[0], values_ref)
    load_z = [load(mamba_hbm.at[1, a:b], mamba_w.at[1, a:b]) for a, b in feat_cuts]
    load_step = load(step_hbm, step_w)
    chan_cuts = cuts_of(channels, 512)
    load_out = [load(out_hbm.at[a:b], out_w.at[a:b]) for a, b in chan_cuts]
    load_attn = load(attn_hbm, attn_w)

    if spread_ffn:
        grp = lax.axis_index("req")
        units = down_hbm.shape[1]
        last = -(-units // tile) - 1
        place = jnp.minimum(grp, last)
        ffn_loads = []
        for p in range(tile // LANES):
            avail = min(LANES, units - last * tile - p * LANES)
            window = pl.ds(pl.multiple_of(place * tile + p * LANES, LANES), LANES)
            piece = slice(p * LANES, (p + 1) * LANES)
            first = 24 + 4 * p
            full = [
                pltpu.make_async_copy(
                    gate_up_hbm.at[:, :, window], gate_up_w.at[:, :, piece], load_sem.at[first]
                ),
                pltpu.make_async_copy(
                    down_hbm.at[:, window], down_w.at[:, piece], load_sem.at[first + 1]
                ),
            ]
            tail = []
            if 0 < avail < LANES:
                end = slice(units - avail, units)
                tail = [
                    pltpu.make_async_copy(
                        gate_up_hbm.at[:, :, end], gate_up_tail, load_sem.at[first + 2]
                    ),
                    pltpu.make_async_copy(down_hbm.at[:, end], down_tail, load_sem.at[first + 3]),
                ]
            ffn_loads.append((avail, piece, full, tail))

        def each_load(act):
            for avail, piece, full, tail in ffn_loads:
                if avail == LANES:
                    for copy in full:
                        act(copy)
                    continue

                @pl.when(grp < last)
                def _():
                    for copy in full:
                        act(copy)

                if tail:

                    @pl.when(grp >= last)
                    def _():
                        for copy in tail:
                            act(copy)

        each_load(lambda copy: copy.start())

    barrier = pltpu.get_barrier_semaphore()
    for k in range(1, count):
        pl.semaphore_signal(
            barrier, inc=1, device_id={"blk": lax.rem(me + k, count)}, device_id_type=MESH
        )
    if spread_ffn:

        @pl.loop(1, groups)
        def _(k):
            for b in range(count):
                pl.semaphore_signal(
                    barrier, inc=1, device_id=(lax.rem(grp + k, groups), b), device_id_type=MESH
                )

        pl.semaphore_wait(barrier, groups * count - 1)
    else:
        pl.semaphore_wait(barrier, count - 1)

    hidden_f = hidden_ref[...].astype(jnp.float32)
    normed_f = hidden_f * rms_scale(hidden_f) * norm_ref[...].reshape(1, width)
    own_feat = own_part(normed_f, me, count).astype(jnp.bfloat16)
    normed = normed_f.astype(jnp.bfloat16)

    load_qkv.wait()
    qkv_buf[me] = row_dot(own_feat, qkv_w[...])
    sent_qkv = send_all(qkv_buf, send_sem, recv_sem, 0, count)

    def feature_dot(which, waits):
        result = jnp.zeros((1, channels), jnp.float32)
        for (a, b), wait in zip(feat_cuts, waits):
            wait.wait()
            result = result + row_dot(normed[:, a:b], mamba_w[which, a:b])
        return result

    inner_act = silu(feature_dot(0, load_x)).astype(jnp.bfloat16)
    inner_f = inner_act.astype(jnp.float32)
    load_select.wait()
    sel_buf[me] = bdot_t(jnp.broadcast_to(inner_act, (ROWS, channels)), select_w[...])[0:1]
    sent_sel = send_all(sel_buf, send_sem, recv_sem, 1, count)

    wait_all(sent_qkv, qkv_buf, send_sem, recv_sem, 0, count)
    qkv_f = total_of(qkv_buf, count).astype(jnp.bfloat16).astype(jnp.float32)
    fresh_ref[...] = qkv_f[:, att_width:].astype(jnp.bfloat16)
    query = qkv_f[:, :att_width]
    new_key = qkv_f[:, att_width : att_width + key_width]
    new_value = qkv_f[:, att_width + key_width :]

    def owner_column(flat):
        head_group = jnp.zeros_like(flat)
        for g in range(1, KEY_HEADS):
            head_group = head_group + (flat >= g * group * HEAD_SIZE).astype(jnp.int32)
        return head_group * HEAD_SIZE + (flat & (HEAD_SIZE - 1))

    flat_rows = lax.broadcasted_iota(jnp.int32, (att_width, key_width), 0)
    flat_cols = lax.broadcasted_iota(jnp.int32, (att_width, key_width), 1)
    spread = (owner_column(flat_rows) == flat_cols).astype(jnp.float32).astype(jnp.bfloat16)
    head_of = lax.broadcasted_iota(jnp.int32, (HEAD_ROWS, att_width), 0)
    head_lane = lax.broadcasted_iota(jnp.int32, (HEAD_ROWS, att_width), 1)
    query_rows = jnp.where(head_of == (head_lane >> 6), jnp.broadcast_to(query, head_of.shape), 0.0)
    query_f = bdot(query_rows.astype(jnp.bfloat16), spread)
    query_bf = query_f.astype(jnp.bfloat16)

    scale = HEAD_SIZE ** (-0.5)
    load_keys.wait()
    scores = bdot(query_bf, keys_ref[...]) * scale
    lane = lax.broadcasted_iota(jnp.int32, (1, positions), 1)
    kept = jnp.zeros((1, positions), jnp.int32)
    for j in range(positions // BLOCK_POSITIONS):
        kept = jnp.where((lane >> 7) == j, keep_ref[0, j], kept)
    limit = length_ref[0] - me * positions
    live = jnp.where(lane < limit, kept, 0) == 1
    live = jnp.broadcast_to(live, scores.shape)
    masked = jnp.where(live, scores, floor_score)
    local_max = jnp.max(masked, axis=-1, keepdims=True)
    weights = jnp.where(live, jnp.exp(masked - local_max), 0.0)
    local_sum = jnp.sum(weights, axis=-1, keepdims=True)
    load_values.wait()
    stat_buf[me, :, :key_width] = bdot_t(weights.astype(jnp.bfloat16), values_ref[...])
    stat_lane = lax.broadcasted_iota(jnp.int32, (HEAD_ROWS, 128), 1)
    stat_buf[me, :, STAT_LANES - 128 :] = jnp.where(stat_lane < 64, local_max, local_sum)
    sent_stat = send_all(stat_buf, send_sem, recv_sem, 2, count)

    z_act = silu(feature_dot(1, load_z))

    wait_all(sent_sel, sel_buf, send_sem, recv_sem, 1, count)
    select_full = total_of(sel_buf, count)
    low = select_full[:, :RANK]
    low_a = low.astype(jnp.bfloat16).astype(jnp.float32)
    low_b = (low - low_a).astype(jnp.bfloat16).astype(jnp.float32)
    low_c = low - low_a - low_b
    term = lax.broadcasted_iota(jnp.int32, (ROWS, RANK), 0)
    terms = jnp.where(term == 0, low_a, jnp.where(term == 1, low_b, jnp.where(term == 2, low_c, 0.0)))
    load_step.wait()
    step_rows = bdot(terms.astype(jnp.bfloat16), step_w[...])
    raw = step_rows[0:1] + step_rows[1:2] + step_rows[2:3] + bias_ref[...].reshape(1, channels)
    step_size = jnp.maximum(raw, 0.0) + jnp.log1p(jnp.exp(-jnp.abs(raw)))

    gain_rows = lax.broadcasted_iota(jnp.int32, (NS, RANK + 2 * NS), 0)
    gain_lane = lax.broadcasted_iota(jnp.int32, (NS, RANK + 2 * NS), 1)
    select_rows = jnp.broadcast_to(select_full, gain_rows.shape)
    in_gain = jnp.sum(
        jnp.where(gain_lane == gain_rows + RANK, select_rows, 0.0), axis=1, keepdims=True
    )
    out_gain = jnp.sum(
        jnp.where(gain_lane == gain_rows + (RANK + NS), select_rows, 0.0), axis=1, keepdims=True
    )
    decay = jnp.exp(-step_size * jnp.exp(decay_ref[...]))
    new_state = decay * state_ref[0] + (step_size * inner_f) * in_gain
    new_state_ref[0] = new_state
    ssm_out = jnp.sum(out_gain * new_state, axis=0, keepdims=True)
    ssm_out = ssm_out + skip_ref[...].reshape(1, channels) * inner_f
    mamba_act = (ssm_out * z_act).astype(jnp.bfloat16)
    mix = jnp.zeros((1, width), jnp.float32)
    for (a, b), wait in zip(chan_cuts, load_out):
        wait.wait()
        mix = mix + row_dot(mamba_act[:, a:b], out_w[a:b])

    wait_all(sent_stat, stat_buf, send_sem, recv_sem, 2, count)
    own_score = jnp.sum(query_f * new_key, axis=-1, keepdims=True) * scale
    highest = own_score
    for k in range(count):
        highest = jnp.maximum(highest, stat_buf[k, :, STAT_LANES - 128 : STAT_LANES - 127])
    total = jnp.zeros_like(own_score)
    accum = jnp.zeros((HEAD_ROWS, key_width), jnp.float32)
    for k in range(count):
        factor = jnp.exp(stat_buf[k, :, STAT_LANES - 128 : STAT_LANES - 127] - highest)
        total = total + stat_buf[k, :, STAT_LANES - 64 : STAT_LANES - 63] * factor
        accum = accum + stat_buf[k, :, :key_width] * factor
    own_weight = jnp.exp(own_score - highest)
    total = total + own_weight
    accum = accum + own_weight * new_value
    attended = accum / total
    att_rows = lax.broadcasted_iota(jnp.int32, attended.shape, 0)
    att_cols = lax.broadcasted_iota(jnp.int32, attended.shape, 1) >> 6
    att_group = jnp.zeros_like(att_rows)
    for g in range(1, KEY_HEADS):
        att_group = att_group + (att_rows >= g * group).astype(jnp.int32)
    attended = jnp.where(att_group == att_cols, attended, 0.0).astype(jnp.bfloat16)
    part = att_width // count
    gather_rows = lax.broadcasted_iota(jnp.int32, (key_width, part), 0)
    gather_cols = lax.broadcasted_iota(jnp.int32, (key_width, part), 1) + me * part
    gather = (owner_column(gather_cols) == gather_rows).astype(jnp.float32).astype(jnp.bfloat16)
    att_flat = bdot(attended, gather)
    flat_head = lax.broadcasted_iota(jnp.int32, (HEAD_ROWS, part), 0)
    flat_lane = (lax.broadcasted_iota(jnp.int32, (HEAD_ROWS, part), 1) + me * part) >> 6
    own_att = jnp.sum(jnp.where(flat_head == flat_lane, att_flat, 0.0), axis=0, keepdims=True)
    load_attn.wait()
    mix = mix + row_dot(own_att.astype(jnp.bfloat16), attn_w[...])
    mix_buf[me] = 0.5 * mix
    sent_mix = send_all(mix_buf, send_sem, recv_sem, 3, count)
    wait_all(sent_mix, mix_buf, send_sem, recv_sem, 3, count)
    resid = (hidden_f + total_of(mix_buf, count)).astype(jnp.bfloat16)
    if not spread_ffn:
        resid_ref[...] = resid
        return

    row_buf[grp] = resid.astype(jnp.float32)

    @pl.loop(1, groups)
    def _(k):
        pltpu.make_async_remote_copy(
            src_ref=row_buf.at[grp],
            dst_ref=row_buf.at[grp],
            send_sem=far_send.at[0],
            recv_sem=far_recv.at[0],
            device_id=(lax.rem(grp + k, groups), me),
            device_id_type=MESH,
        ).start()

    lane = lax.broadcasted_iota(jnp.int32, (groups, groups), 1)
    slots = jnp.zeros((groups, groups), jnp.int32)
    for s in range(groups):
        slots = jnp.where(lane == s, slot_ref[s], slots)
    request = lax.broadcasted_iota(jnp.int32, (groups, groups), 0)
    picker = (slots == request).astype(jnp.float32).astype(jnp.bfloat16)
    each_load(lambda copy: copy.wait())
    for avail, piece, _, tail in ffn_loads:
        if avail == LANES:
            continue

        @pl.when(grp >= last)
        def _():
            gate_up_w[:, :, piece] = jnp.zeros_like(gate_up_w[:, :, piece])
            down_w[:, piece] = jnp.zeros_like(down_w[:, piece])
            if tail:
                begin = piece.start
                gate_up_w[:, :, begin : begin + avail] = gate_up_tail[...]
                down_w[:, begin : begin + avail] = down_tail[...]

    def far_wait(stage, buf, amount):
        return pltpu.make_async_remote_copy(
            src_ref=buf.at[pl.ds(0, amount)],
            dst_ref=buf.at[pl.ds(0, amount)],
            send_sem=far_send.at[stage],
            recv_sem=far_recv.at[stage],
            device_id=(lax.rem(grp + 1, groups), me),
            device_id_type=MESH,
        )

    far_wait(0, row_buf, groups - 1).wait_recv()
    for r in range(groups):
        rows_ref[r : r + 1, :] = row_buf[r]
    resid_f = rows_ref[...]
    ffn_in = (resid_f * rms_scale(resid_f) * gain_ref[...].reshape(1, width)).astype(jnp.bfloat16)
    unit = grp * tile + lax.broadcasted_iota(jnp.int32, (groups, tile), 1)
    ffn_hidden = silu(bdot(ffn_in, gate_up_w[0])) * bdot(ffn_in, gate_up_w[1])
    ffn_hidden = jnp.where(unit < units, ffn_hidden, 0.0).astype(jnp.bfloat16)
    placed = bdot(picker, ffn_hidden).astype(jnp.bfloat16)
    terms = bdot_t(placed, down_w[...])
    half = width // count
    for b in range(count):
        piece = terms[:, b * half : (b + 1) * half]
        for r in range(groups):
            part_buf[b, r] = piece[r : r + 1]
    slot = grp * count + me

    def part_send(peer, blk):
        pltpu.make_async_remote_copy(
            src_ref=part_buf.at[blk, peer],
            dst_ref=take_buf.at[slot],
            send_sem=far_send.at[1],
            recv_sem=far_recv.at[1],
            device_id=(peer, blk),
            device_id_type=MESH,
        ).start()

    @pl.loop(1, groups)
    def _(k):
        for b in range(count):
            part_send(lax.rem(grp + k, groups), b)

    for k in range(1, count):
        part_send(grp, lax.rem(me + k, count))
    take_buf[slot] = part_buf[me, grp]
    rows_ref[...] = bdot(picker, resid_f.astype(jnp.bfloat16))
    own_row = own_part(rows_ref[pl.ds(grp, 1), :], me, count)
    amount = groups * count - 1
    far_wait(1, take_buf, amount).wait_recv()
    resid_ref[...] = (own_row + jnp.sum(take_buf[...], axis=0)).astype(jnp.bfloat16)
    far_wait(0, row_buf, groups - 1).wait_send()
    far_wait(1, take_buf, amount).wait_send()


def layer(
    hidden, cache_length, block_keep, stored_keys, stored_values, ssm_state, norm_gain,
    query_key_value_weight, w_attn_out, mamba_in, select_proj, step_proj, step_bias, decay_log,
    skip_gain, w_mamba_out, ffn_gain, slot_request, w_gate_up, w_down, spread_ffn,
):
    count = lax.axis_size("blk")
    width = hidden.shape[1]
    channels = ssm_state.shape[2]
    qkv_width = query_key_value_weight.shape[1]
    vmem = pl.BlockSpec(memory_space=pltpu.VMEM)
    smem = pl.BlockSpec(memory_space=pltpu.SMEM)
    hbm = pl.BlockSpec(memory_space=pl.ANY)
    stored_keys, stored_values, select_proj = (
        jnp.swapaxes(a, -1, -2) for a in (stored_keys, stored_values, select_proj)
    )
    big = (query_key_value_weight, w_attn_out, mamba_in, select_proj, step_proj, w_mamba_out)
    groups = lax.axis_size("req")
    units = w_down.shape[0]
    tile = -(-units // (groups * LANES)) * LANES
    ffn_args, ffn_specs, ffn_scratch = [], [], []
    if spread_ffn:
        tail = units % LANES or LANES
        half = width // count
        ffn_args = [ffn_gain, slot_request, w_gate_up, w_down.T]
        ffn_specs = [vmem, smem, hbm, hbm]
        ffn_scratch = [
            pltpu.VMEM((2, width, tile), jnp.bfloat16),
            pltpu.VMEM((width, tile), jnp.bfloat16),
            pltpu.VMEM((2, width, tail), jnp.bfloat16),
            pltpu.VMEM((width, tail), jnp.bfloat16),
            pltpu.VMEM((groups, 1, width), jnp.float32),
            pltpu.VMEM((groups, width), jnp.float32),
            pltpu.VMEM((count, groups, 1, half), jnp.float32),
            pltpu.VMEM((groups * count, 1, half), jnp.float32),
            pltpu.SemaphoreType.DMA((2,)),
            pltpu.SemaphoreType.DMA((2,)),
        ]
    return pl.pallas_call(
        partial(layer_kernel, count, groups, tile, spread_ffn),
        out_shape=(
            jax.ShapeDtypeStruct((1, width // count if spread_ffn else width), jnp.bfloat16),
            jax.ShapeDtypeStruct((1, 2 * KEY_HEADS * HEAD_SIZE), jnp.bfloat16),
            jax.ShapeDtypeStruct(ssm_state.shape, jnp.float32),
        ),
        in_specs=[vmem, smem, smem, vmem, vmem, vmem, vmem, vmem] + [hbm] * 8 + ffn_specs,
        out_specs=(vmem, vmem, vmem),
        scratch_shapes=[
            pltpu.VMEM(stored_keys.shape[1:], jnp.bfloat16),
            pltpu.VMEM(stored_values.shape[1:], jnp.bfloat16),
        ]
        + [pltpu.VMEM(w.shape, w.dtype) for w in big]
        + [
            pltpu.VMEM((count, 1, qkv_width), jnp.float32),
            pltpu.VMEM((count, 1, select_proj.shape[0]), jnp.float32),
            pltpu.VMEM((count, HEAD_ROWS, STAT_LANES), jnp.float32),
            pltpu.VMEM((count, 1, width), jnp.float32),
            pltpu.SemaphoreType.DMA((40,)),
            pltpu.SemaphoreType.DMA((4, count)),
            pltpu.SemaphoreType.DMA((4, count)),
        ]
        + ffn_scratch,
        compiler_params=pltpu.CompilerParams(
            collective_id=0, has_side_effects=True, vmem_limit_bytes=VMEM_BYTES
        ),
    )(
        hidden, cache_length, block_keep, ssm_state, norm_gain, step_bias, decay_log, skip_gain,
        stored_keys, stored_values, *big, *ffn_args,
    )


def ffn_plain(resid, ffn_gain, slot_request, w_gate_up, w_down):
    blk_index = lax.axis_index("blk")
    grp_index = lax.axis_index("req")
    resid_f = resid.astype(jnp.float32)
    ffn_in = (resid_f * rms_scale(resid_f) * ffn_gain).astype(jnp.bfloat16)
    ffn_hidden = (silu(bdot(ffn_in, w_gate_up[0])) * bdot(ffn_in, w_gate_up[1])).astype(
        jnp.bfloat16
    )
    ffn_out = lax.psum(bdot(ffn_hidden, w_down), "blk")
    final_rows = (resid_f + ffn_out).astype(jnp.bfloat16)
    every_row = lax.all_gather(final_rows, "req", axis=0, tiled=True)
    part = resid.shape[1] // lax.axis_size("blk")
    columns = lax.dynamic_slice_in_dim(every_row, blk_index * part, part, 1)
    picker = (slot_request[None, :] == grp_index).astype(jnp.bfloat16)
    return bdot(picker, columns).astype(jnp.bfloat16)


def per_device(
    hidden,
    slot_request,
    cache_length,
    block_keep,
    stored_keys,
    stored_values,
    ssm_state,
    norm_gain,
    query_key_value_weight,
    w_attn_out,
    mamba_in,
    select_proj,
    step_proj,
    step_bias,
    decay_log,
    skip_gain,
    w_mamba_out,
    ffn_gain,
    w_gate_up,
    w_down,
):
    spread_ffn = lax.axis_size("req") <= 16
    row, fresh_entry, new_state = layer(
        hidden, cache_length, block_keep, stored_keys, stored_values, ssm_state, norm_gain,
        query_key_value_weight, w_attn_out, mamba_in, select_proj, step_proj, step_bias,
        decay_log, skip_gain, w_mamba_out, ffn_gain, slot_request, w_gate_up, w_down, spread_ffn,
    )
    if not spread_ffn:
        row = ffn_plain(row, ffn_gain, slot_request, w_gate_up, w_down)
    return (row, fresh_entry, new_state)


def solution(mesh):
    return jax.shard_map(
        per_device,
        mesh=mesh,
        in_specs=(
            P("req", None),
            P(),
            P("req"),
            P("req", "blk"),
            P("req", "blk", None),
            P("req", "blk", None),
            P("req", None, "blk"),
            P(),
            P("blk", None),
            P("blk", None),
            P(None, None, "blk"),
            P("blk", None),
            P(None, "blk"),
            P("blk"),
            P(None, "blk"),
            P("blk"),
            P("blk", None),
            P(),
            P(None, None, "blk"),
            P("blk", None),
        ),
        out_specs=(P("req", "blk"), P("req", None), P("req", None, "blk")),
        check_vma=False,
    )
```

```python
from functools import partial

import jax
import jax.numpy as jnp
from jax import lax
from jax.experimental import pallas as pl
from jax.experimental.pallas import tpu as pltpu
from jax.sharding import PartitionSpec as P

QUERY_HEADS = 25
HEAD_SIZE = 64
KEY_HEADS = 5
NS = 16
RANK = 100
BLOCK_POSITIONS = 128


epsilon = 1e-05
floor_score = -1e30

MESH = pl.DeviceIdType.MESH
VMEM_BYTES = 60 * 1024 * 1024
ROWS = 16
HEAD_ROWS = 32
STAT_LANES = 512
LANES = 128


def rms_scale(block_values):
    return lax.rsqrt(jnp.mean(block_values * block_values, axis=-1, keepdims=True) + epsilon)


def silu(value):
    return value * jax.nn.sigmoid(value)


def bdot(left, right):
    return jnp.dot(left, right, preferred_element_type=jnp.float32)


def bdot_t(left, right):
    return lax.dot_general(
        left, right, (((1,), (1,)), ((), ())), preferred_element_type=jnp.float32
    )


def row_dot(row, weight):
    tall = jnp.broadcast_to(row, (ROWS, row.shape[1]))
    return bdot(tall, weight)[0:1]


def cuts_of(total, step):
    edges = list(range(0, total, step)) + [total]
    if len(edges) > 2 and edges[-1] - edges[-2] < step // 2:
        edges.pop(-2)
    return list(zip(edges[:-1], edges[1:]))


def own_part(value, index, count):
    width = value.shape[1] // count
    part = value[:, :width]
    for other in range(1, count):
        part = jnp.where(index == other, value[:, other * width : (other + 1) * width], part)
    return part


def send_all(buf, send_sem, recv_sem, stage, count):
    me = lax.axis_index("blk")
    copies = []
    for k in range(1, count):
        target = lax.rem(me + k, count)
        copy = pltpu.make_async_remote_copy(
            src_ref=buf.at[me],
            dst_ref=buf.at[me],
            send_sem=send_sem.at[stage, k],
            recv_sem=recv_sem.at[stage, me],
            device_id={"blk": target},
            device_id_type=MESH,
        )
        copy.start()
        copies.append(copy)
    return copies


def wait_all(copies, buf, send_sem, recv_sem, stage, count):
    me = lax.axis_index("blk")
    for k in range(1, count):
        source = lax.rem(me + k, count)
        pltpu.make_async_remote_copy(
            src_ref=buf.at[source],
            dst_ref=buf.at[source],
            send_sem=send_sem.at[stage, k],
            recv_sem=recv_sem.at[stage, source],
            device_id={"blk": source},
            device_id_type=MESH,
        ).wait_recv()
    for copy in copies:
        copy.wait_send()


def total_of(buf, count):
    result = buf[0]
    for k in range(1, count):
        result = result + buf[k]
    return result


def layer_kernel(
    count,
    groups,
    tile,
    spread_ffn,
    *refs,
):
    (
        hidden_ref, length_ref, keep_ref, state_ref, norm_ref, bias_ref, decay_ref, skip_ref,
        keys_hbm, values_hbm, qkv_hbm, attn_hbm, mamba_hbm, select_hbm, step_hbm, out_hbm,
    ) = refs[:16]
    refs = refs[16:]
    if spread_ffn:
        gain_ref, slot_ref, gate_up_hbm, down_hbm = refs[:4]
        refs = refs[4:]
    resid_ref, fresh_ref, new_state_ref = refs[:3]
    (
        keys_ref, values_ref, qkv_w, attn_w, mamba_w, select_w, step_w, out_w,
        qkv_buf, sel_buf, stat_buf, mix_buf, load_sem, send_sem, recv_sem,
    ) = refs[3:18]
    if spread_ffn:
        (
            gate_up_w, down_w, gate_up_tail, down_tail, row_buf, rows_ref, part_buf, take_buf,
            far_send, far_recv,
        ) = refs[18:]
    me = lax.axis_index("blk")
    width = hidden_ref.shape[1]
    channels = state_ref.shape[2]
    positions = keys_ref.shape[1]
    key_width = KEY_HEADS * HEAD_SIZE
    group = QUERY_HEADS // KEY_HEADS
    att_width = QUERY_HEADS * HEAD_SIZE
    loads = []

    def load(source, target):
        copy = pltpu.make_async_copy(source, target, load_sem.at[len(loads)])
        copy.start()
        loads.append(copy)
        return copy

    feat_cuts = cuts_of(width, 512)
    load_qkv = load(qkv_hbm, qkv_w)
    load_x = [load(mamba_hbm.at[0, a:b], mamba_w.at[0, a:b]) for a, b in feat_cuts]
    load_select = load(select_hbm, select_w)
    load_keys = load(keys_hbm.at[0], keys_ref)
    load_values = load(values_hbm.at[0], values_ref)
    load_z = [load(mamba_hbm.at[1, a:b], mamba_w.at[1, a:b]) for a, b in feat_cuts]
    load_step = load(step_hbm, step_w)
    chan_cuts = cuts_of(channels, 512)
    load_out = [load(out_hbm.at[a:b], out_w.at[a:b]) for a, b in chan_cuts]
    load_attn = load(attn_hbm, attn_w)

    if spread_ffn:
        grp = lax.axis_index("req")
        units = down_hbm.shape[1]
        last = -(-units // tile) - 1
        place = jnp.minimum(grp, last)
        ffn_loads = []
        for p in range(tile // LANES):
            avail = min(LANES, units - last * tile - p * LANES)
            window = pl.ds(pl.multiple_of(place * tile + p * LANES, LANES), LANES)
            piece = slice(p * LANES, (p + 1) * LANES)
            first = 24 + 4 * p
            full = [
                pltpu.make_async_copy(
                    gate_up_hbm.at[:, :, window], gate_up_w.at[:, :, piece], load_sem.at[first]
                ),
                pltpu.make_async_copy(
                    down_hbm.at[:, window], down_w.at[:, piece], load_sem.at[first + 1]
                ),
            ]
            tail = []
            if 0 < avail < LANES:
                end = slice(units - avail, units)
                tail = [
                    pltpu.make_async_copy(
                        gate_up_hbm.at[:, :, end], gate_up_tail, load_sem.at[first + 2]
                    ),
                    pltpu.make_async_copy(down_hbm.at[:, end], down_tail, load_sem.at[first + 3]),
                ]
            ffn_loads.append((avail, piece, full, tail))

        def each_load(act):
            for avail, piece, full, tail in ffn_loads:
                if avail == LANES:
                    for copy in full:
                        act(copy)
                    continue

                @pl.when(grp < last)
                def _():
                    for copy in full:
                        act(copy)

                if tail:

                    @pl.when(grp >= last)
                    def _():
                        for copy in tail:
                            act(copy)

        each_load(lambda copy: copy.start())

    barrier = pltpu.get_barrier_semaphore()
    for k in range(1, count):
        pl.semaphore_signal(
            barrier, inc=1, device_id={"blk": lax.rem(me + k, count)}, device_id_type=MESH
        )
    if spread_ffn:

        @pl.loop(1, groups)
        def _(k):
            for b in range(count):
                pl.semaphore_signal(
                    barrier, inc=1, device_id=(lax.rem(grp + k, groups), b), device_id_type=MESH
                )

        pl.semaphore_wait(barrier, groups * count - 1)
    else:
        pl.semaphore_wait(barrier, count - 1)

    hidden_f = hidden_ref[...].astype(jnp.float32)
    normed_f = hidden_f * rms_scale(hidden_f) * norm_ref[...].reshape(1, width)
    own_feat = own_part(normed_f, me, count).astype(jnp.bfloat16)
    normed = normed_f.astype(jnp.bfloat16)

    load_qkv.wait()
    qkv_buf[me] = row_dot(own_feat, qkv_w[...])
    sent_qkv = send_all(qkv_buf, send_sem, recv_sem, 0, count)

    def feature_dot(which, waits):
        result = jnp.zeros((1, channels), jnp.float32)
        for (a, b), wait in zip(feat_cuts, waits):
            wait.wait()
            result = result + row_dot(normed[:, a:b], mamba_w[which, a:b])
        return result

    inner_act = silu(feature_dot(0, load_x)).astype(jnp.bfloat16)
    inner_f = inner_act.astype(jnp.float32)
    load_select.wait()
    sel_buf[me] = bdot_t(jnp.broadcast_to(inner_act, (ROWS, channels)), select_w[...])[0:1]
    sent_sel = send_all(sel_buf, send_sem, recv_sem, 1, count)

    wait_all(sent_qkv, qkv_buf, send_sem, recv_sem, 0, count)
    qkv_f = total_of(qkv_buf, count).astype(jnp.bfloat16).astype(jnp.float32)
    fresh_ref[...] = qkv_f[:, att_width:].astype(jnp.bfloat16)
    query = qkv_f[:, :att_width]
    new_key = qkv_f[:, att_width : att_width + key_width]
    new_value = qkv_f[:, att_width + key_width :]

    def owner_column(flat):
        head_group = jnp.zeros_like(flat)
        for g in range(1, KEY_HEADS):
            head_group = head_group + (flat >= g * group * HEAD_SIZE).astype(jnp.int32)
        return head_group * HEAD_SIZE + (flat & (HEAD_SIZE - 1))

    flat_rows = lax.broadcasted_iota(jnp.int32, (att_width, key_width), 0)
    flat_cols = lax.broadcasted_iota(jnp.int32, (att_width, key_width), 1)
    spread = (owner_column(flat_rows) == flat_cols).astype(jnp.float32).astype(jnp.bfloat16)
    head_of = lax.broadcasted_iota(jnp.int32, (HEAD_ROWS, att_width), 0)
    head_lane = lax.broadcasted_iota(jnp.int32, (HEAD_ROWS, att_width), 1)
    query_rows = jnp.where(head_of == (head_lane >> 6), jnp.broadcast_to(query, head_of.shape), 0.0)
    query_f = bdot(query_rows.astype(jnp.bfloat16), spread)
    query_bf = query_f.astype(jnp.bfloat16)

    scale = HEAD_SIZE ** (-0.5)
    load_keys.wait()
    scores = bdot(query_bf, keys_ref[...]) * scale
    lane = lax.broadcasted_iota(jnp.int32, (1, positions), 1)
    kept = jnp.zeros((1, positions), jnp.int32)
    for j in range(positions // BLOCK_POSITIONS):
        kept = jnp.where((lane >> 7) == j, keep_ref[0, j], kept)
    limit = length_ref[0] - me * positions
    live = jnp.where(lane < limit, kept, 0) == 1
    live = jnp.broadcast_to(live, scores.shape)
    masked = jnp.where(live, scores, floor_score)
    local_max = jnp.max(masked, axis=-1, keepdims=True)
    weights = jnp.where(live, jnp.exp(masked - local_max), 0.0)
    local_sum = jnp.sum(weights, axis=-1, keepdims=True)
    load_values.wait()
    stat_buf[me, :, :key_width] = bdot_t(weights.astype(jnp.bfloat16), values_ref[...])
    stat_lane = lax.broadcasted_iota(jnp.int32, (HEAD_ROWS, 128), 1)
    stat_buf[me, :, STAT_LANES - 128 :] = jnp.where(stat_lane < 64, local_max, local_sum)
    sent_stat = send_all(stat_buf, send_sem, recv_sem, 2, count)

    z_act = silu(feature_dot(1, load_z))

    wait_all(sent_sel, sel_buf, send_sem, recv_sem, 1, count)
    select_full = total_of(sel_buf, count)
    low = select_full[:, :RANK]
    low_a = low.astype(jnp.bfloat16).astype(jnp.float32)
    low_b = (low - low_a).astype(jnp.bfloat16).astype(jnp.float32)
    low_c = low - low_a - low_b
    term = lax.broadcasted_iota(jnp.int32, (ROWS, RANK), 0)
    terms = jnp.where(term == 0, low_a, jnp.where(term == 1, low_b, jnp.where(term == 2, low_c, 0.0)))
    load_step.wait()
    step_rows = bdot(terms.astype(jnp.bfloat16), step_w[...])
    raw = step_rows[0:1] + step_rows[1:2] + step_rows[2:3] + bias_ref[...].reshape(1, channels)
    step_size = jnp.maximum(raw, 0.0) + jnp.log1p(jnp.exp(-jnp.abs(raw)))

    gain_rows = lax.broadcasted_iota(jnp.int32, (NS, RANK + 2 * NS), 0)
    gain_lane = lax.broadcasted_iota(jnp.int32, (NS, RANK + 2 * NS), 1)
    select_rows = jnp.broadcast_to(select_full, gain_rows.shape)
    in_gain = jnp.sum(
        jnp.where(gain_lane == gain_rows + RANK, select_rows, 0.0), axis=1, keepdims=True
    )
    out_gain = jnp.sum(
        jnp.where(gain_lane == gain_rows + (RANK + NS), select_rows, 0.0), axis=1, keepdims=True
    )
    decay = jnp.exp(-step_size * jnp.exp(decay_ref[...]))
    new_state = decay * state_ref[0] + (step_size * inner_f) * in_gain
    new_state_ref[0] = new_state
    ssm_out = jnp.sum(out_gain * new_state, axis=0, keepdims=True)
    ssm_out = ssm_out + skip_ref[...].reshape(1, channels) * inner_f
    mamba_act = (ssm_out * z_act).astype(jnp.bfloat16)
    mix = jnp.zeros((1, width), jnp.float32)
    for (a, b), wait in zip(chan_cuts, load_out):
        wait.wait()
        mix = mix + row_dot(mamba_act[:, a:b], out_w[a:b])

    wait_all(sent_stat, stat_buf, send_sem, recv_sem, 2, count)
    own_score = jnp.sum(query_f * new_key, axis=-1, keepdims=True) * scale
    highest = own_score
    for k in range(count):
        highest = jnp.maximum(highest, stat_buf[k, :, STAT_LANES - 128 : STAT_LANES - 127])
    total = jnp.zeros_like(own_score)
    accum = jnp.zeros((HEAD_ROWS, key_width), jnp.float32)
    for k in range(count):
        factor = jnp.exp(stat_buf[k, :, STAT_LANES - 128 : STAT_LANES - 127] - highest)
        total = total + stat_buf[k, :, STAT_LANES - 64 : STAT_LANES - 63] * factor
        accum = accum + stat_buf[k, :, :key_width] * factor
    own_weight = jnp.exp(own_score - highest)
    total = total + own_weight
    accum = accum + own_weight * new_value
    attended = accum / total
    att_rows = lax.broadcasted_iota(jnp.int32, attended.shape, 0)
    att_cols = lax.broadcasted_iota(jnp.int32, attended.shape, 1) >> 6
    att_group = jnp.zeros_like(att_rows)
    for g in range(1, KEY_HEADS):
        att_group = att_group + (att_rows >= g * group).astype(jnp.int32)
    attended = jnp.where(att_group == att_cols, attended, 0.0).astype(jnp.bfloat16)
    part = att_width // count
    gather_rows = lax.broadcasted_iota(jnp.int32, (key_width, part), 0)
    gather_cols = lax.broadcasted_iota(jnp.int32, (key_width, part), 1) + me * part
    gather = (owner_column(gather_cols) == gather_rows).astype(jnp.float32).astype(jnp.bfloat16)
    att_flat = bdot(attended, gather)
    flat_head = lax.broadcasted_iota(jnp.int32, (HEAD_ROWS, part), 0)
    flat_lane = (lax.broadcasted_iota(jnp.int32, (HEAD_ROWS, part), 1) + me * part) >> 6
    own_att = jnp.sum(jnp.where(flat_head == flat_lane, att_flat, 0.0), axis=0, keepdims=True)
    load_attn.wait()
    mix = mix + row_dot(own_att.astype(jnp.bfloat16), attn_w[...])
    mix_buf[me] = 0.5 * mix
    sent_mix = send_all(mix_buf, send_sem, recv_sem, 3, count)
    wait_all(sent_mix, mix_buf, send_sem, recv_sem, 3, count)
    resid = (hidden_f + total_of(mix_buf, count)).astype(jnp.bfloat16)
    if not spread_ffn:
        resid_ref[...] = resid
        return

    row_buf[grp] = resid

    @pl.loop(1, groups)
    def _(k):
        pltpu.make_async_remote_copy(
            src_ref=row_buf.at[grp],
            dst_ref=row_buf.at[grp],
            send_sem=far_send.at[0],
            recv_sem=far_recv.at[0],
            device_id=(lax.rem(grp + k, groups), me),
            device_id_type=MESH,
        ).start()

    lane = lax.broadcasted_iota(jnp.int32, (groups, groups), 1)
    slots = jnp.zeros((groups, groups), jnp.int32)
    for s in range(groups):
        slots = jnp.where(lane == s, slot_ref[s], slots)
    request = lax.broadcasted_iota(jnp.int32, (groups, groups), 0)
    picker = (slots == request).astype(jnp.float32).astype(jnp.bfloat16)
    each_load(lambda copy: copy.wait())
    for avail, piece, _, tail in ffn_loads:
        if avail == LANES:
            continue

        @pl.when(grp >= last)
        def _():
            gate_up_w[:, :, piece] = jnp.zeros_like(gate_up_w[:, :, piece])
            down_w[:, piece] = jnp.zeros_like(down_w[:, piece])
            if tail:
                begin = piece.start
                gate_up_w[:, :, begin : begin + avail] = gate_up_tail[...]
                down_w[:, begin : begin + avail] = down_tail[...]

    def far_wait(stage, buf, amount):
        return pltpu.make_async_remote_copy(
            src_ref=buf.at[pl.ds(0, amount)],
            dst_ref=buf.at[pl.ds(0, amount)],
            send_sem=far_send.at[stage],
            recv_sem=far_recv.at[stage],
            device_id=(lax.rem(grp + 1, groups), me),
            device_id_type=MESH,
        )

    far_wait(0, row_buf, groups - 1).wait_recv()
    for r in range(groups):
        rows_ref[r : r + 1, :] = row_buf[r].astype(jnp.float32)
    resid_f = rows_ref[...]
    ffn_in = (resid_f * rms_scale(resid_f) * gain_ref[...].reshape(1, width)).astype(jnp.bfloat16)
    half = width // count
    slot = grp * count + me
    senders = (last + 1) * count

    def part_send(peer, blk):
        pltpu.make_async_remote_copy(
            src_ref=part_buf.at[blk, peer],
            dst_ref=take_buf.at[slot],
            send_sem=far_send.at[1],
            recv_sem=far_recv.at[1],
            device_id=(peer, blk),
            device_id_type=MESH,
        ).start()

    @pl.when(grp <= last)
    def _():
        unit = grp * tile + lax.broadcasted_iota(jnp.int32, (groups, tile), 1)
        ffn_hidden = silu(bdot(ffn_in, gate_up_w[0])) * bdot(ffn_in, gate_up_w[1])
        ffn_hidden = jnp.where(unit < units, ffn_hidden, 0.0).astype(jnp.bfloat16)
        placed = bdot(picker, ffn_hidden).astype(jnp.bfloat16)
        terms = bdot_t(placed, down_w[...])
        for b in range(count):
            piece = terms[:, b * half : (b + 1) * half]
            for r in range(groups):
                part_buf[b, r] = piece[r : r + 1].astype(jnp.bfloat16)

        @pl.loop(1, groups)
        def _(k):
            for b in range(count):
                part_send(lax.rem(grp + k, groups), b)

        for k in range(1, count):
            part_send(grp, lax.rem(me + k, count))
        take_buf[slot] = part_buf[me, grp]

    rows_ref[...] = bdot(picker, resid_f.astype(jnp.bfloat16))
    own_row = own_part(rows_ref[pl.ds(grp, 1), :], me, count)

    @pl.when(grp <= last)
    def _():
        far_wait(1, take_buf, senders - 1).wait_recv()

    @pl.when(grp > last)
    def _():
        far_wait(1, take_buf, senders).wait_recv()

    result = own_row
    for k in range(senders):
        result = result + take_buf[k].astype(jnp.float32)
    resid_ref[...] = result.astype(jnp.bfloat16)
    far_wait(0, row_buf, groups - 1).wait_send()

    @pl.when(grp <= last)
    def _():
        far_wait(1, take_buf, groups * count - 1).wait_send()


def hand_over_kernel(row_in, fresh_in, state_in, row_out, fresh_out, state_out):
    row_out[...] = row_in[...]
    fresh_out[...] = fresh_in[...]
    state_out[...] = state_in[...]


def hand_over(*results):
    vmem = pl.BlockSpec(memory_space=pltpu.VMEM)
    return pl.pallas_call(
        hand_over_kernel,
        out_shape=tuple(jax.ShapeDtypeStruct(r.shape, r.dtype) for r in results),
        in_specs=[vmem] * 3,
        out_specs=(vmem,) * 3,
    )(*results)


def layer(
    hidden, cache_length, block_keep, stored_keys, stored_values, ssm_state, norm_gain,
    query_key_value_weight, w_attn_out, mamba_in, select_proj, step_proj, step_bias, decay_log,
    skip_gain, w_mamba_out, ffn_gain, slot_request, w_gate_up, w_down, spread_ffn,
):
    count = lax.axis_size("blk")
    width = hidden.shape[1]
    channels = ssm_state.shape[2]
    qkv_width = query_key_value_weight.shape[1]
    vmem = pl.BlockSpec(memory_space=pltpu.VMEM)
    smem = pl.BlockSpec(memory_space=pltpu.SMEM)
    hbm = pl.BlockSpec(memory_space=pl.ANY)
    stored_keys, stored_values, select_proj = (
        jnp.swapaxes(a, -1, -2) for a in (stored_keys, stored_values, select_proj)
    )
    big = (query_key_value_weight, w_attn_out, mamba_in, select_proj, step_proj, w_mamba_out)
    groups = lax.axis_size("req")
    units = w_down.shape[0]
    tile = -(-units // (groups * LANES)) * LANES
    ffn_args, ffn_specs, ffn_scratch = [], [], []
    if spread_ffn:
        tail = units % LANES or LANES
        half = width // count
        ffn_args = [ffn_gain, slot_request, w_gate_up, w_down.T]
        ffn_specs = [vmem, smem, hbm, hbm]
        ffn_scratch = [
            pltpu.VMEM((2, width, tile), jnp.bfloat16),
            pltpu.VMEM((width, tile), jnp.bfloat16),
            pltpu.VMEM((2, width, tail), jnp.bfloat16),
            pltpu.VMEM((width, tail), jnp.bfloat16),
            pltpu.VMEM((groups, 1, width), jnp.bfloat16),
            pltpu.VMEM((groups, width), jnp.float32),
            pltpu.VMEM((count, groups, 1, half), jnp.bfloat16),
            pltpu.VMEM((groups * count, 1, half), jnp.bfloat16),
            pltpu.SemaphoreType.DMA((2,)),
            pltpu.SemaphoreType.DMA((2,)),
        ]
    return pl.pallas_call(
        partial(layer_kernel, count, groups, tile, spread_ffn),
        out_shape=(
            jax.ShapeDtypeStruct((1, width // count if spread_ffn else width), jnp.bfloat16),
            jax.ShapeDtypeStruct((1, 2 * KEY_HEADS * HEAD_SIZE), jnp.bfloat16),
            jax.ShapeDtypeStruct(ssm_state.shape, jnp.float32),
        ),
        in_specs=[vmem, smem, smem, vmem, vmem, vmem, vmem, vmem] + [hbm] * 8 + ffn_specs,
        out_specs=(vmem, vmem, vmem),
        scratch_shapes=[
            pltpu.VMEM(stored_keys.shape[1:], jnp.bfloat16),
            pltpu.VMEM(stored_values.shape[1:], jnp.bfloat16),
        ]
        + [pltpu.VMEM(w.shape, w.dtype) for w in big]
        + [
            pltpu.VMEM((count, 1, qkv_width), jnp.float32),
            pltpu.VMEM((count, 1, select_proj.shape[0]), jnp.float32),
            pltpu.VMEM((count, HEAD_ROWS, STAT_LANES), jnp.float32),
            pltpu.VMEM((count, 1, width), jnp.float32),
            pltpu.SemaphoreType.DMA((40,)),
            pltpu.SemaphoreType.DMA((4, count)),
            pltpu.SemaphoreType.DMA((4, count)),
        ]
        + ffn_scratch,
        compiler_params=pltpu.CompilerParams(
            collective_id=0, has_side_effects=True, vmem_limit_bytes=VMEM_BYTES
        ),
    )(
        hidden, cache_length, block_keep, ssm_state, norm_gain, step_bias, decay_log, skip_gain,
        stored_keys, stored_values, *big, *ffn_args,
    )


def ffn_plain(resid, ffn_gain, slot_request, w_gate_up, w_down):
    blk_index = lax.axis_index("blk")
    grp_index = lax.axis_index("req")
    resid_f = resid.astype(jnp.float32)
    ffn_in = (resid_f * rms_scale(resid_f) * ffn_gain).astype(jnp.bfloat16)
    ffn_hidden = (silu(bdot(ffn_in, w_gate_up[0])) * bdot(ffn_in, w_gate_up[1])).astype(
        jnp.bfloat16
    )
    ffn_out = lax.psum(bdot(ffn_hidden, w_down), "blk")
    final_rows = (resid_f + ffn_out).astype(jnp.bfloat16)
    every_row = lax.all_gather(final_rows, "req", axis=0, tiled=True)
    part = resid.shape[1] // lax.axis_size("blk")
    columns = lax.dynamic_slice_in_dim(every_row, blk_index * part, part, 1)
    picker = (slot_request[None, :] == grp_index).astype(jnp.bfloat16)
    return bdot(picker, columns).astype(jnp.bfloat16)


def per_device(
    hidden,
    slot_request,
    cache_length,
    block_keep,
    stored_keys,
    stored_values,
    ssm_state,
    norm_gain,
    query_key_value_weight,
    w_attn_out,
    mamba_in,
    select_proj,
    step_proj,
    step_bias,
    decay_log,
    skip_gain,
    w_mamba_out,
    ffn_gain,
    w_gate_up,
    w_down,
):
    spread_ffn = lax.axis_size("req") <= 16
    row, fresh_entry, new_state = layer(
        hidden, cache_length, block_keep, stored_keys, stored_values, ssm_state, norm_gain,
        query_key_value_weight, w_attn_out, mamba_in, select_proj, step_proj, step_bias,
        decay_log, skip_gain, w_mamba_out, ffn_gain, slot_request, w_gate_up, w_down, spread_ffn,
    )
    if not spread_ffn:
        row = ffn_plain(row, ffn_gain, slot_request, w_gate_up, w_down)
    return hand_over(row, fresh_entry, new_state)


def solution(mesh):
    return jax.shard_map(
        per_device,
        mesh=mesh,
        in_specs=(
            P("req", None),
            P(),
            P("req"),
            P("req", "blk"),
            P("req", "blk", None),
            P("req", "blk", None),
            P("req", None, "blk"),
            P(),
            P("blk", None),
            P("blk", None),
            P(None, None, "blk"),
            P("blk", None),
            P(None, "blk"),
            P("blk"),
            P(None, "blk"),
            P("blk"),
            P("blk", None),
            P(),
            P(None, None, "blk"),
            P("blk", None),
        ),
        out_specs=(P("req", "blk"), P("req", None), P("req", None, "blk")),
        check_vma=False,
    )
```

```python
from functools import partial

import jax
import jax.numpy as jnp
from jax import lax
from jax.experimental import pallas as pl
from jax.experimental.pallas import tpu as pltpu
from jax.sharding import PartitionSpec as P

QUERY_HEADS = 25
HEAD_SIZE = 64
KEY_HEADS = 5
NS = 16
RANK = 100
BLOCK_POSITIONS = 128


epsilon = 1e-05
floor_score = -1e30

MESH = pl.DeviceIdType.MESH
VMEM_BYTES = 60 * 1024 * 1024
ROWS = 16
HEAD_ROWS = 32
STAT_LANES = 512
LANES = 128


def rms_scale(block_values):
    return lax.rsqrt(jnp.mean(block_values * block_values, axis=-1, keepdims=True) + epsilon)


def silu(value):
    return value * jax.nn.sigmoid(value)


def bdot(left, right):
    return jnp.dot(left, right, preferred_element_type=jnp.float32)


def bdot_t(left, right):
    return lax.dot_general(
        left, right, (((1,), (1,)), ((), ())), preferred_element_type=jnp.float32
    )


def row_dot(row, weight):
    tall = jnp.broadcast_to(row, (ROWS, row.shape[1]))
    return bdot(tall, weight)[0:1]


def cuts_of(total, step):
    edges = list(range(0, total, step)) + [total]
    if len(edges) > 2 and edges[-1] - edges[-2] < step // 2:
        edges.pop(-2)
    return list(zip(edges[:-1], edges[1:]))


def own_part(value, index, count):
    width = value.shape[1] // count
    part = value[:, :width]
    for other in range(1, count):
        part = jnp.where(index == other, value[:, other * width : (other + 1) * width], part)
    return part


def send_all(buf, send_sem, recv_sem, stage, count):
    me = lax.axis_index("blk")
    copies = []
    for k in range(1, count):
        target = lax.rem(me + k, count)
        copy = pltpu.make_async_remote_copy(
            src_ref=buf.at[me],
            dst_ref=buf.at[me],
            send_sem=send_sem.at[stage, k],
            recv_sem=recv_sem.at[stage, me],
            device_id={"blk": target},
            device_id_type=MESH,
        )
        copy.start()
        copies.append(copy)
    return copies


def wait_all(copies, buf, send_sem, recv_sem, stage, count):
    me = lax.axis_index("blk")
    for k in range(1, count):
        source = lax.rem(me + k, count)
        pltpu.make_async_remote_copy(
            src_ref=buf.at[source],
            dst_ref=buf.at[source],
            send_sem=send_sem.at[stage, k],
            recv_sem=recv_sem.at[stage, source],
            device_id={"blk": source},
            device_id_type=MESH,
        ).wait_recv()
    for copy in copies:
        copy.wait_send()


def total_of(buf, count):
    result = buf[0]
    for k in range(1, count):
        result = result + buf[k]
    return result


def layer_kernel(
    count,
    groups,
    tile,
    spread_ffn,
    *refs,
):
    (
        hidden_ref, length_ref, keep_ref, state_ref, norm_ref, bias_ref, decay_ref, skip_ref,
        keys_hbm, values_hbm, qkv_hbm, attn_hbm, mamba_hbm, select_hbm, step_hbm, out_hbm,
    ) = refs[:16]
    refs = refs[16:]
    if spread_ffn:
        gain_ref, slot_ref, gate_up_hbm, down_hbm = refs[:4]
        refs = refs[4:]
    resid_ref, fresh_ref, new_state_ref = refs[:3]
    (
        keys_ref, values_ref, qkv_w, attn_w, mamba_w, select_w, step_w, out_w,
        qkv_buf, sel_buf, stat_buf, mix_buf, spread_ref, gather_ref, load_sem, send_sem, recv_sem,
    ) = refs[3:20]
    if spread_ffn:
        (
            gate_up_w, down_w, gate_up_tail, down_tail, row_buf, rows_ref, part_buf, take_buf,
            far_send, far_recv,
        ) = refs[20:]
    me = lax.axis_index("blk")
    width = hidden_ref.shape[1]
    channels = state_ref.shape[2]
    positions = keys_ref.shape[1]
    key_width = KEY_HEADS * HEAD_SIZE
    group = QUERY_HEADS // KEY_HEADS
    att_width = QUERY_HEADS * HEAD_SIZE
    loads = []

    def load(source, target):
        copy = pltpu.make_async_copy(source, target, load_sem.at[len(loads)])
        copy.start()
        loads.append(copy)
        return copy

    feat_cuts = cuts_of(width, 512)
    load_qkv = load(qkv_hbm, qkv_w)
    load_x = [load(mamba_hbm.at[0, a:b], mamba_w.at[0, a:b]) for a, b in feat_cuts]
    load_select = load(select_hbm, select_w)
    load_keys = load(keys_hbm.at[0], keys_ref)
    load_values = load(values_hbm.at[0], values_ref)
    load_z = [load(mamba_hbm.at[1, a:b], mamba_w.at[1, a:b]) for a, b in feat_cuts]
    load_step = load(step_hbm, step_w)
    chan_cuts = cuts_of(channels, 512)
    load_out = [load(out_hbm.at[a:b], out_w.at[a:b]) for a, b in chan_cuts]
    load_attn = load(attn_hbm, attn_w)

    if spread_ffn:
        grp = lax.axis_index("req")
        units = down_hbm.shape[1]
        last = -(-units // tile) - 1
        place = jnp.minimum(grp, last)
        ffn_loads = []
        for p in range(tile // LANES):
            avail = min(LANES, units - last * tile - p * LANES)
            window = pl.ds(pl.multiple_of(place * tile + p * LANES, LANES), LANES)
            piece = slice(p * LANES, (p + 1) * LANES)
            first = 24 + 4 * p
            full = [
                pltpu.make_async_copy(
                    gate_up_hbm.at[:, :, window], gate_up_w.at[:, :, piece], load_sem.at[first]
                ),
                pltpu.make_async_copy(
                    down_hbm.at[:, window], down_w.at[:, piece], load_sem.at[first + 1]
                ),
            ]
            tail = []
            if 0 < avail < LANES:
                end = slice(units - avail, units)
                tail = [
                    pltpu.make_async_copy(
                        gate_up_hbm.at[:, :, end], gate_up_tail, load_sem.at[first + 2]
                    ),
                    pltpu.make_async_copy(down_hbm.at[:, end], down_tail, load_sem.at[first + 3]),
                ]
            ffn_loads.append((avail, piece, full, tail))

        def each_load(act):
            for avail, piece, full, tail in ffn_loads:
                if avail == LANES:
                    for copy in full:
                        act(copy)
                    continue

                @pl.when(grp < last)
                def _():
                    for copy in full:
                        act(copy)

                if tail:

                    @pl.when(grp >= last)
                    def _():
                        for copy in tail:
                            act(copy)

        each_load(lambda copy: copy.start())

    barrier = pltpu.get_barrier_semaphore()
    for k in range(1, count):
        pl.semaphore_signal(
            barrier, inc=1, device_id={"blk": lax.rem(me + k, count)}, device_id_type=MESH
        )
    if spread_ffn:

        @pl.loop(1, groups)
        def _(k):
            for b in range(count):
                pl.semaphore_signal(
                    barrier, inc=1, device_id=(lax.rem(grp + k, groups), b), device_id_type=MESH
                )


    part = att_width // count
    def owner_column(flat):
        head_group = jnp.zeros_like(flat)
        for g in range(1, KEY_HEADS):
            head_group = head_group + (flat >= g * group * HEAD_SIZE).astype(jnp.int32)
        return head_group * HEAD_SIZE + (flat & (HEAD_SIZE - 1))

    def selection(first, amount):
        owner = owner_column(lax.broadcasted_iota(jnp.int32, (1, amount), 1) + first)
        row = lax.broadcasted_iota(jnp.int32, (key_width, amount), 0)
        return jnp.where(row == owner, 1.0, 0.0).astype(jnp.bfloat16)

    spread_ref[...] = selection(0, att_width)
    gather_ref[...] = selection(me * part, part)

    hidden_f = hidden_ref[...].astype(jnp.float32)
    normed_f = hidden_f * rms_scale(hidden_f) * norm_ref[...].reshape(1, width)
    own_feat = own_part(normed_f, me, count).astype(jnp.bfloat16)
    normed = normed_f.astype(jnp.bfloat16)

    load_qkv.wait()
    qkv_buf[me] = row_dot(own_feat, qkv_w[...])
    pl.semaphore_wait(barrier, groups * count - 1 if spread_ffn else count - 1)
    sent_qkv = send_all(qkv_buf, send_sem, recv_sem, 0, count)

    def feature_dot(which, waits):
        result = jnp.zeros((1, channels), jnp.float32)
        for (a, b), wait in zip(feat_cuts, waits):
            wait.wait()
            result = result + row_dot(normed[:, a:b], mamba_w[which, a:b])
        return result

    inner_act = silu(feature_dot(0, load_x)).astype(jnp.bfloat16)
    inner_f = inner_act.astype(jnp.float32)
    load_select.wait()
    sel_buf[me] = bdot_t(jnp.broadcast_to(inner_act, (ROWS, channels)), select_w[...])[0:1]
    sent_sel = send_all(sel_buf, send_sem, recv_sem, 1, count)

    wait_all(sent_qkv, qkv_buf, send_sem, recv_sem, 0, count)
    qkv_f = total_of(qkv_buf, count).astype(jnp.bfloat16).astype(jnp.float32)
    fresh_ref[...] = qkv_f[:, att_width:].astype(jnp.bfloat16)
    query = qkv_f[:, :att_width]
    new_key = qkv_f[:, att_width : att_width + key_width]
    new_value = qkv_f[:, att_width + key_width :]

    head_of = lax.broadcasted_iota(jnp.int32, (HEAD_ROWS, att_width), 0)
    head_lane = lax.broadcasted_iota(jnp.int32, (HEAD_ROWS, att_width), 1)
    query_rows = jnp.where(head_of == (head_lane >> 6), jnp.broadcast_to(query, head_of.shape), 0.0)
    query_f = bdot_t(query_rows.astype(jnp.bfloat16), spread_ref[...])
    query_bf = query_f.astype(jnp.bfloat16)

    scale = HEAD_SIZE ** (-0.5)
    load_keys.wait()
    scores = bdot(query_bf, keys_ref[...]) * scale
    lane = lax.broadcasted_iota(jnp.int32, (1, positions), 1)
    kept = jnp.zeros((1, positions), jnp.int32)
    for j in range(positions // BLOCK_POSITIONS):
        kept = jnp.where((lane >> 7) == j, keep_ref[0, j], kept)
    limit = length_ref[0] - me * positions
    live = jnp.where(lane < limit, kept, 0) == 1
    live = jnp.broadcast_to(live, scores.shape)
    masked = jnp.where(live, scores, floor_score)
    local_max = jnp.max(masked, axis=-1, keepdims=True)
    weights = jnp.where(live, jnp.exp(masked - local_max), 0.0)
    local_sum = jnp.sum(weights, axis=-1, keepdims=True)
    load_values.wait()
    stat_buf[me, :, :key_width] = bdot_t(weights.astype(jnp.bfloat16), values_ref[...])
    stat_lane = lax.broadcasted_iota(jnp.int32, (HEAD_ROWS, 128), 1)
    stat_buf[me, :, STAT_LANES - 128 :] = jnp.where(stat_lane < 64, local_max, local_sum)
    sent_stat = send_all(stat_buf, send_sem, recv_sem, 2, count)

    z_act = silu(feature_dot(1, load_z))

    wait_all(sent_sel, sel_buf, send_sem, recv_sem, 1, count)
    select_full = total_of(sel_buf, count)
    low = select_full[:, :RANK]
    low_a = low.astype(jnp.bfloat16).astype(jnp.float32)
    low_b = (low - low_a).astype(jnp.bfloat16).astype(jnp.float32)
    low_c = low - low_a - low_b
    term = lax.broadcasted_iota(jnp.int32, (ROWS, RANK), 0)
    terms = jnp.where(term == 0, low_a, jnp.where(term == 1, low_b, jnp.where(term == 2, low_c, 0.0)))
    load_step.wait()
    step_rows = bdot(terms.astype(jnp.bfloat16), step_w[...])
    raw = step_rows[0:1] + step_rows[1:2] + step_rows[2:3] + bias_ref[...].reshape(1, channels)
    step_size = jnp.maximum(raw, 0.0) + jnp.log1p(jnp.exp(-jnp.abs(raw)))

    gain_rows = lax.broadcasted_iota(jnp.int32, (NS, RANK + 2 * NS), 0)
    gain_lane = lax.broadcasted_iota(jnp.int32, (NS, RANK + 2 * NS), 1)
    select_rows = jnp.broadcast_to(select_full, gain_rows.shape)
    in_gain = jnp.sum(
        jnp.where(gain_lane == gain_rows + RANK, select_rows, 0.0), axis=1, keepdims=True
    )
    out_gain = jnp.sum(
        jnp.where(gain_lane == gain_rows + (RANK + NS), select_rows, 0.0), axis=1, keepdims=True
    )
    decay = jnp.exp(-step_size * jnp.exp(decay_ref[...]))
    new_state = decay * state_ref[0] + (step_size * inner_f) * in_gain
    new_state_ref[0] = new_state
    ssm_out = jnp.sum(out_gain * new_state, axis=0, keepdims=True)
    ssm_out = ssm_out + skip_ref[...].reshape(1, channels) * inner_f
    mamba_act = (ssm_out * z_act).astype(jnp.bfloat16)
    mix = jnp.zeros((1, width), jnp.float32)
    for (a, b), wait in zip(chan_cuts, load_out):
        wait.wait()
        mix = mix + row_dot(mamba_act[:, a:b], out_w[a:b])

    wait_all(sent_stat, stat_buf, send_sem, recv_sem, 2, count)
    own_score = jnp.sum(query_f * new_key, axis=-1, keepdims=True) * scale
    highest = own_score
    for k in range(count):
        highest = jnp.maximum(highest, stat_buf[k, :, STAT_LANES - 128 : STAT_LANES - 127])
    total = jnp.zeros_like(own_score)
    accum = jnp.zeros((HEAD_ROWS, key_width), jnp.float32)
    for k in range(count):
        factor = jnp.exp(stat_buf[k, :, STAT_LANES - 128 : STAT_LANES - 127] - highest)
        total = total + stat_buf[k, :, STAT_LANES - 64 : STAT_LANES - 63] * factor
        accum = accum + stat_buf[k, :, :key_width] * factor
    own_weight = jnp.exp(own_score - highest)
    total = total + own_weight
    accum = accum + own_weight * new_value
    attended = accum / total
    att_rows = lax.broadcasted_iota(jnp.int32, attended.shape, 0)
    att_cols = lax.broadcasted_iota(jnp.int32, attended.shape, 1) >> 6
    att_group = jnp.zeros_like(att_rows)
    for g in range(1, KEY_HEADS):
        att_group = att_group + (att_rows >= g * group).astype(jnp.int32)
    attended = jnp.where(att_group == att_cols, attended, 0.0).astype(jnp.bfloat16)
    att_flat = bdot(attended, gather_ref[...])
    flat_head = lax.broadcasted_iota(jnp.int32, (HEAD_ROWS, part), 0)
    flat_lane = (lax.broadcasted_iota(jnp.int32, (HEAD_ROWS, part), 1) + me * part) >> 6
    own_att = jnp.sum(jnp.where(flat_head == flat_lane, att_flat, 0.0), axis=0, keepdims=True)
    load_attn.wait()
    mix = mix + row_dot(own_att.astype(jnp.bfloat16), attn_w[...])
    mix_buf[me] = 0.5 * mix
    sent_mix = send_all(mix_buf, send_sem, recv_sem, 3, count)
    wait_all(sent_mix, mix_buf, send_sem, recv_sem, 3, count)
    resid = (hidden_f + total_of(mix_buf, count)).astype(jnp.bfloat16)
    if not spread_ffn:
        resid_ref[...] = resid
        return

    row_buf[grp] = resid

    @pl.loop(1, groups)
    def _(k):
        pltpu.make_async_remote_copy(
            src_ref=row_buf.at[grp],
            dst_ref=row_buf.at[grp],
            send_sem=far_send.at[0],
            recv_sem=far_recv.at[0],
            device_id=(lax.rem(grp + k, groups), me),
            device_id_type=MESH,
        ).start()

    lane = lax.broadcasted_iota(jnp.int32, (groups, groups), 1)
    slots = jnp.zeros((groups, groups), jnp.int32)
    for s in range(groups):
        slots = jnp.where(lane == s, slot_ref[s], slots)
    request = lax.broadcasted_iota(jnp.int32, (groups, groups), 0)
    picker = (slots == request).astype(jnp.float32).astype(jnp.bfloat16)
    each_load(lambda copy: copy.wait())
    for avail, piece, _, tail in ffn_loads:
        if avail == LANES:
            continue

        @pl.when(grp >= last)
        def _():
            gate_up_w[:, :, piece] = jnp.zeros_like(gate_up_w[:, :, piece])
            down_w[:, piece] = jnp.zeros_like(down_w[:, piece])
            if tail:
                begin = piece.start
                gate_up_w[:, :, begin : begin + avail] = gate_up_tail[...]
                down_w[:, begin : begin + avail] = down_tail[...]

    def far_wait(stage, buf, amount):
        return pltpu.make_async_remote_copy(
            src_ref=buf.at[pl.ds(0, amount)],
            dst_ref=buf.at[pl.ds(0, amount)],
            send_sem=far_send.at[stage],
            recv_sem=far_recv.at[stage],
            device_id=(lax.rem(grp + 1, groups), me),
            device_id_type=MESH,
        )

    far_wait(0, row_buf, groups - 1).wait_recv()
    for r in range(groups):
        rows_ref[r : r + 1, :] = row_buf[r].astype(jnp.float32)
    resid_f = rows_ref[...]
    ffn_in = (resid_f * rms_scale(resid_f) * gain_ref[...].reshape(1, width)).astype(jnp.bfloat16)
    half = width // count
    slot = grp * count + me
    senders = (last + 1) * count

    def part_send(peer, blk):
        pltpu.make_async_remote_copy(
            src_ref=part_buf.at[blk, peer],
            dst_ref=take_buf.at[slot],
            send_sem=far_send.at[1],
            recv_sem=far_recv.at[1],
            device_id=(peer, blk),
            device_id_type=MESH,
        ).start()

    @pl.when(grp <= last)
    def _():
        unit = grp * tile + lax.broadcasted_iota(jnp.int32, (groups, tile), 1)
        ffn_hidden = silu(bdot(ffn_in, gate_up_w[0])) * bdot(ffn_in, gate_up_w[1])
        ffn_hidden = jnp.where(unit < units, ffn_hidden, 0.0).astype(jnp.bfloat16)
        placed = bdot(picker, ffn_hidden).astype(jnp.bfloat16)
        terms = bdot_t(placed, down_w[...])
        for b in range(count):
            piece = terms[:, b * half : (b + 1) * half]
            for r in range(groups):
                part_buf[b, r] = piece[r : r + 1].astype(jnp.bfloat16)

        @pl.loop(1, groups)
        def _(k):
            for b in range(count):
                part_send(lax.rem(grp + k, groups), b)

        for k in range(1, count):
            part_send(grp, lax.rem(me + k, count))
        take_buf[slot] = part_buf[me, grp]

    rows_ref[...] = bdot(picker, resid_f.astype(jnp.bfloat16))
    own_row = own_part(rows_ref[pl.ds(grp, 1), :], me, count)

    @pl.when(grp <= last)
    def _():
        far_wait(1, take_buf, senders - 1).wait_recv()

    @pl.when(grp > last)
    def _():
        far_wait(1, take_buf, senders).wait_recv()

    result = own_row
    for k in range(senders):
        result = result + take_buf[k].astype(jnp.float32)
    resid_ref[...] = result.astype(jnp.bfloat16)
    far_wait(0, row_buf, groups - 1).wait_send()

    @pl.when(grp <= last)
    def _():
        far_wait(1, take_buf, groups * count - 1).wait_send()


def hand_over_kernel(row_in, fresh_in, state_in, row_out, fresh_out, state_out):
    row_out[...] = row_in[...]
    fresh_out[...] = fresh_in[...]
    state_out[...] = state_in[...]


def hand_over(*results):
    vmem = pl.BlockSpec(memory_space=pltpu.VMEM)
    return pl.pallas_call(
        hand_over_kernel,
        out_shape=tuple(jax.ShapeDtypeStruct(r.shape, r.dtype) for r in results),
        in_specs=[vmem] * 3,
        out_specs=(vmem,) * 3,
    )(*results)


def layer(
    hidden, cache_length, block_keep, stored_keys, stored_values, ssm_state, norm_gain,
    query_key_value_weight, w_attn_out, mamba_in, select_proj, step_proj, step_bias, decay_log,
    skip_gain, w_mamba_out, ffn_gain, slot_request, w_gate_up, w_down, spread_ffn,
):
    count = lax.axis_size("blk")
    width = hidden.shape[1]
    channels = ssm_state.shape[2]
    qkv_width = query_key_value_weight.shape[1]
    vmem = pl.BlockSpec(memory_space=pltpu.VMEM)
    smem = pl.BlockSpec(memory_space=pltpu.SMEM)
    hbm = pl.BlockSpec(memory_space=pl.ANY)
    stored_keys, stored_values, select_proj = (
        jnp.swapaxes(a, -1, -2) for a in (stored_keys, stored_values, select_proj)
    )
    big = (query_key_value_weight, w_attn_out, mamba_in, select_proj, step_proj, w_mamba_out)
    groups = lax.axis_size("req")
    units = w_down.shape[0]
    tile = -(-units // (groups * LANES)) * LANES
    ffn_args, ffn_specs, ffn_scratch = [], [], []
    if spread_ffn:
        tail = units % LANES or LANES
        half = width // count
        ffn_args = [ffn_gain, slot_request, w_gate_up, w_down.T]
        ffn_specs = [vmem, smem, hbm, hbm]
        ffn_scratch = [
            pltpu.VMEM((2, width, tile), jnp.bfloat16),
            pltpu.VMEM((width, tile), jnp.bfloat16),
            pltpu.VMEM((2, width, tail), jnp.bfloat16),
            pltpu.VMEM((width, tail), jnp.bfloat16),
            pltpu.VMEM((groups, 1, width), jnp.bfloat16),
            pltpu.VMEM((groups, width), jnp.float32),
            pltpu.VMEM((count, groups, 1, half), jnp.bfloat16),
            pltpu.VMEM((groups * count, 1, half), jnp.bfloat16),
            pltpu.SemaphoreType.DMA((2,)),
            pltpu.SemaphoreType.DMA((2,)),
        ]
    return pl.pallas_call(
        partial(layer_kernel, count, groups, tile, spread_ffn),
        out_shape=(
            jax.ShapeDtypeStruct((1, width // count if spread_ffn else width), jnp.bfloat16),
            jax.ShapeDtypeStruct((1, 2 * KEY_HEADS * HEAD_SIZE), jnp.bfloat16),
            jax.ShapeDtypeStruct(ssm_state.shape, jnp.float32),
        ),
        in_specs=[vmem, smem, smem, vmem, vmem, vmem, vmem, vmem] + [hbm] * 8 + ffn_specs,
        out_specs=(vmem, vmem, vmem),
        scratch_shapes=[
            pltpu.VMEM(stored_keys.shape[1:], jnp.bfloat16),
            pltpu.VMEM(stored_values.shape[1:], jnp.bfloat16),
        ]
        + [pltpu.VMEM(w.shape, w.dtype) for w in big]
        + [
            pltpu.VMEM((count, 1, qkv_width), jnp.float32),
            pltpu.VMEM((count, 1, select_proj.shape[0]), jnp.float32),
            pltpu.VMEM((count, HEAD_ROWS, STAT_LANES), jnp.float32),
            pltpu.VMEM((count, 1, width), jnp.float32),
            pltpu.VMEM((KEY_HEADS * HEAD_SIZE, QUERY_HEADS * HEAD_SIZE), jnp.bfloat16),
            pltpu.VMEM((KEY_HEADS * HEAD_SIZE, QUERY_HEADS * HEAD_SIZE // count), jnp.bfloat16),
            pltpu.SemaphoreType.DMA((40,)),
            pltpu.SemaphoreType.DMA((4, count)),
            pltpu.SemaphoreType.DMA((4, count)),
        ]
        + ffn_scratch,
        compiler_params=pltpu.CompilerParams(
            collective_id=0, has_side_effects=True, vmem_limit_bytes=VMEM_BYTES
        ),
    )(
        hidden, cache_length, block_keep, ssm_state, norm_gain, step_bias, decay_log, skip_gain,
        stored_keys, stored_values, *big, *ffn_args,
    )


def ffn_plain(resid, ffn_gain, slot_request, w_gate_up, w_down):
    blk_index = lax.axis_index("blk")
    grp_index = lax.axis_index("req")
    resid_f = resid.astype(jnp.float32)
    ffn_in = (resid_f * rms_scale(resid_f) * ffn_gain).astype(jnp.bfloat16)
    ffn_hidden = (silu(bdot(ffn_in, w_gate_up[0])) * bdot(ffn_in, w_gate_up[1])).astype(
        jnp.bfloat16
    )
    ffn_out = lax.psum(bdot(ffn_hidden, w_down), "blk")
    final_rows = (resid_f + ffn_out).astype(jnp.bfloat16)
    every_row = lax.all_gather(final_rows, "req", axis=0, tiled=True)
    part = resid.shape[1] // lax.axis_size("blk")
    columns = lax.dynamic_slice_in_dim(every_row, blk_index * part, part, 1)
    picker = (slot_request[None, :] == grp_index).astype(jnp.bfloat16)
    return bdot(picker, columns).astype(jnp.bfloat16)


def per_device(
    hidden,
    slot_request,
    cache_length,
    block_keep,
    stored_keys,
    stored_values,
    ssm_state,
    norm_gain,
    query_key_value_weight,
    w_attn_out,
    mamba_in,
    select_proj,
    step_proj,
    step_bias,
    decay_log,
    skip_gain,
    w_mamba_out,
    ffn_gain,
    w_gate_up,
    w_down,
):
    spread_ffn = lax.axis_size("req") <= 16
    row, fresh_entry, new_state = layer(
        hidden, cache_length, block_keep, stored_keys, stored_values, ssm_state, norm_gain,
        query_key_value_weight, w_attn_out, mamba_in, select_proj, step_proj, step_bias,
        decay_log, skip_gain, w_mamba_out, ffn_gain, slot_request, w_gate_up, w_down, spread_ffn,
    )
    if not spread_ffn:
        row = ffn_plain(row, ffn_gain, slot_request, w_gate_up, w_down)
    return hand_over(row, fresh_entry, new_state)


def solution(mesh):
    return jax.shard_map(
        per_device,
        mesh=mesh,
        in_specs=(
            P("req", None),
            P(),
            P("req"),
            P("req", "blk"),
            P("req", "blk", None),
            P("req", "blk", None),
            P("req", None, "blk"),
            P(),
            P("blk", None),
            P("blk", None),
            P(None, None, "blk"),
            P("blk", None),
            P(None, "blk"),
            P("blk"),
            P(None, "blk"),
            P("blk"),
            P("blk", None),
            P(),
            P(None, None, "blk"),
            P("blk", None),
        ),
        out_specs=(P("req", "blk"), P("req", None), P("req", None, "blk")),
        check_vma=False,
    )
```
